128 devices in a mesh: dp: 16 (over z_hi, x, core), tensor: 8 (over z_lo, y).
Axes of the slice: x: 4, y: 4, z: 4 (z_hi: 2, z_lo: 2; z = z_hi * 2 + z_lo), core: 2. Of those that a mesh axis runs over, the one named last changes fastest.
Arguments:
- tokens: bfloat16 [16384, 8192], P('dp', 'tensor'), may hold values from -6 to 6
- ref_gain: float32 [8192], P('tensor'), may hold values from 0.1 to 1.9
- ref_weight: bfloat16 [8192, 512], P('tensor'), may hold values from -0.0625 to 0.0625
- pol_gain: float32 [8192], replicated, may hold values from 0.1 to 1.9
- pol_weight: bfloat16 [8192, 512], P('dp'), may hold values from -0.0625 to 0.0625
- lengths: int32 [16, 8, 16], P('dp', 'tensor'), may hold values from 1 to 16, 128 in all within a row
- bins: int32 [16, 8, 16], P('dp', 'tensor'), may hold values from 0 to 15, each once within a row
- advantage: float32 [16, 8, 16], P('dp', 'tensor'), may hold values from -4 to 4
- logprob_gap: float32 [16384], P(('dp', 'tensor')), may hold values from -1 to 1
- cotangent: bfloat16 [16, 8, 256, 512], P('dp', 'tensor'), may hold values from -6 to 6
Outputs:
- policy_values: bfloat16 [16, 8, 256, 512], P('dp', 'tensor')
- grad_weight: float32 [8192, 512], P(('dp', 'tensor'))
The draws below stay inside these ranges and needn't reach their ends.
Inputs may be any that keep to these rules, and one draw needn't show every extreme that they name: `lengths`: lengths of the 16 sequences of one run, in the order in which they lie in it; they sum to 128, and the longest of every run is exactly 16. The sequences of one run go to distinct bins: each bin takes exactly one sequence of every run.
All inputs are finite; a program needn't handle non-finite values.
Results may differ from the reference program's by a relative error of at most 0.015.
Values may be sent and summed in bfloat16 or wider, within the bound.
A program may use at most 64 MiB of HBM per device.

```python
import math
import jax
import jax.numpy as jnp
import numpy as np
from jax import lax

D = 8192
VW = 512
TOK_DEV = 128
BINS = 16
TP_WAYS = 8
BLOCK = 1024
SPAN = 16
SLOTS = 256
SEQS = 2048
TOKENS = 16384


def spiked(entries, key, source, target, blocks, factor):
    owner, partner = [(jnp.arange(entries.shape[position]) // (entries.shape[position] // blocks)).reshape([-1 if axis == position else 1 for axis in range(entries.ndim)]) for position in (source, target)]
    chosen = jax.random.permutation(key, blocks)[partner]
    strong = (owner == chosen) | (owner == (partner + blocks // 2) % blocks)
    return jnp.where(strong, factor * entries, entries)


def block_levels(rng, extent, split, smallest, largest):
    def one(dim, blocks):
        steps = jax.random.uniform(jax.random.fold_in(jax.random.fold_in(rng, 6), dim), (blocks,), jnp.float32, smallest / len(split), largest / len(split))
        return jnp.repeat(jnp.exp(steps), extent[dim] // blocks).reshape((-1,) + (1,) * (len(extent) - dim - 1))

    factor_of = one(*split[0])
    for cut in split[1:]:
        factor_of = factor_of * one(*cut)
    return factor_of


def split_up(count, total, reach, skew):
    weights = [(1 << 20) // math.isqrt(standing ** skew) + 1 for standing in range(2, count + 1)]
    surplus, counts = total - reach - (count - 1), [1] * (count - 1)
    while surplus > 0:
        free = [i for i in range(count - 1) if counts[i] < reach]
        pool, budget = sum([weights[i] for i in free]), surplus
        for i in free:
            extra = min(reach - counts[i], max(1, budget * weights[i] // pool), surplus)
            counts[i] = counts[i] + extra
            surplus = surplus - extra
    return np.array([reach] + counts)


def uneven(key, number_of, total, reach, skew):
    if number_of == 2:
        one = jax.random.randint(key, (), max(1, total - reach), min(reach, total - 1) + 1)
        return jnp.stack([one, total - one])
    sizes = jnp.asarray(split_up(number_of, total, reach, skew), jnp.int32)
    pairs = (number_of - 1) // 2
    giver, sink = sizes[1:1 + 2 * pairs:2], sizes[2:2 + 2 * pairs:2]
    slack = jnp.minimum(giver - 1, reach - sink)
    moved = jax.random.randint(jax.random.fold_in(key, 1), (pairs,), 0, 1 << 20) % (slack + 1)
    sizes = sizes.at[1:1 + 2 * pairs:2].set(giver - moved).at[2:2 + 2 * pairs:2].set(sink + moved)
    return sizes[jax.random.permutation(jax.random.fold_in(key, 2), number_of)]


def scatter_about(own_key, shape, width, most, cuts=(), kind=jnp.bfloat16):
    level = block_levels(own_key, shape, cuts, -0.22, 0.18) if cuts else 1.0
    result = jax.random.normal(own_key, shape, jnp.float32) * width * level
    return jnp.minimum(jnp.maximum(result, -most), most).astype(kind)


def noise_with(key, dims, deviation, most, cuts, heavy, kind=jnp.bfloat16):
    drawn = deviation * jax.random.normal(key, dims, jnp.float32)
    if cuts:
        drawn = drawn * block_levels(key, dims, cuts, -0.22, 0.18)
    return jnp.clip(spiked(drawn, jax.random.fold_in(key, 3), *heavy), -most, most).astype(kind)


def setup_inputs(seed: int = 0) -> dict:
    arg_keys = jax.random.split(jax.random.key(seed), 11)
    return {
        "tokens": noise_with(arg_keys[0], (TOKENS, D), 1.0, 6.0, ((0, 16), (1, 8)), (0, 1, 16, 2.0)),
        "ref_gain": jnp.clip(1.0 + 0.18 * jax.random.normal(arg_keys[1], (D,), jnp.float32), 0.1, 1.9),
        "ref_weight": scatter_about(arg_keys[2], (D, VW), D ** -0.5, 0.0625, ((0, 8),)),
        "pol_gain": jnp.clip(1.0 + 0.18 * jax.random.normal(arg_keys[3], (D,), jnp.float32), 0.1, 1.9),
        "pol_weight": scatter_about(arg_keys[4], (D, VW), D ** -0.5, 0.0625, ((0, 16),)),
        "lengths": jax.vmap(lambda own: uneven(own, BINS, TOK_DEV, SPAN, 2))(jax.random.split(arg_keys[5], BINS * TP_WAYS)).reshape((BINS, TP_WAYS, BINS)).astype(jnp.int32),
        "bins": jax.vmap(lambda own: jax.random.permutation(own, BINS))(jax.random.split(arg_keys[6], BINS * TP_WAYS)).reshape((BINS, TP_WAYS, BINS)).astype(jnp.int32),
        "advantage": scatter_about(arg_keys[7], (BINS, TP_WAYS, BINS), 1.0, 4.0, ((0, 16), (1, 8)), jnp.float32),
        "logprob_gap": jnp.clip(jax.random.uniform(arg_keys[8], (TOKENS,), jnp.float32, -1.0, 1.0) * block_levels(arg_keys[8], (TOKENS,), ((0, 128),), -0.4, 0.0), -1.0, 1.0),
        "cotangent": scatter_about(arg_keys[9], (BINS, TP_WAYS, SLOTS, VW), 1.0, 6.0, ((0, 16), (1, 8))),
    }


EPS = 1e-06
BETA = 1.0

def run_values(run_rows, ref_gain, ref_weight):
    accum = jnp.zeros((run_rows.shape[0], VW), jnp.float32)
    for index in range(D // BLOCK):
        lower = index * BLOCK
        scaled = (run_rows[:, lower:lower + BLOCK].astype(jnp.float32) * ref_gain[lower:lower + BLOCK][None, :]).astype(jnp.bfloat16)
        partial_value = jnp.dot(scaled, ref_weight[lower:lower + BLOCK], preferred_element_type=jnp.float32)
        accum = accum + lax.optimization_barrier(partial_value.astype(jnp.bfloat16)).astype(jnp.float32)
    power = lax.optimization_barrier(jnp.mean(jnp.square(run_rows.astype(jnp.float32)), axis=1))
    return (accum * lax.rsqrt(power + EPS)[:, None]).astype(jnp.bfloat16)

def reference(tokens, ref_gain, ref_weight, pol_gain, pol_weight, lengths, bins, advantage, logprob_gap, cotangent):
    run_rows = tokens.reshape(BINS * TP_WAYS, TOK_DEV, D)
    ref_values = lax.map(lambda stretch_rows: run_values(stretch_rows, ref_gain, ref_weight), run_rows)
    ref_flat = ref_values.reshape(TOKENS, VW)
    seq_start = (jnp.cumsum(lengths, axis=2).astype(jnp.int32) - lengths).astype(jnp.int32)
    chosen = bins[:, :, None, :] == jnp.arange(BINS, dtype=jnp.int32)[None, None, :, None]
    bin_len = lax.optimization_barrier(jnp.sum(jnp.where(chosen, lengths[:, :, None, :], 0), axis=3)).astype(jnp.int32)
    bin_start = lax.optimization_barrier(jnp.sum(jnp.where(chosen, seq_start[:, :, None, :], 0), axis=3)).astype(jnp.int32)
    bin_adv = lax.optimization_barrier(jnp.sum(jnp.where(chosen, advantage[:, :, None, :], jnp.float32(0.0)), axis=3))
    run_index = (jnp.arange(BINS, dtype=jnp.int32)[:, None] * TP_WAYS + jnp.arange(TP_WAYS, dtype=jnp.int32)[None, :]).astype(jnp.int32)
    offsets = jnp.arange(SPAN, dtype=jnp.int32)
    usable = offsets[None, None, None, :] < bin_len[..., None]
    local_row = jnp.clip(bin_start[..., None] + offsets[None, None, None, :], 0, TOK_DEV - 1).astype(jnp.int32)
    source = (run_index[:, :, None, None] * TOK_DEV + local_row).astype(jnp.int32)
    importance = jnp.minimum(jnp.exp(logprob_gap[source]), jnp.float32(2.0))
    len_float = bin_len[..., None].astype(jnp.float32)
    coef_adv = lax.optimization_barrier(jnp.where(usable, bin_adv[..., None] * importance / len_float, jnp.float32(0.0)).astype(jnp.bfloat16))
    coef_pull = lax.optimization_barrier(jnp.where(usable, BETA / len_float, jnp.float32(0.0)).astype(jnp.bfloat16))
    factor = 1.0 / math.sqrt(SEQS)

    def pick(array, bin_index):
        return jnp.transpose(array[:, :, bin_index], (1, 0, 2)).reshape(TP_WAYS * SLOTS)

    def per_bin(accum, bin_index):
        src_rows = pick(source, bin_index)
        use_rows = pick(usable, bin_index)
        adv_rows = pick(coef_adv, bin_index).astype(jnp.float32)[:, None]
        pull_rows = pick(coef_pull, bin_index).astype(jnp.float32)[:, None]
        packed_rows = jnp.where(use_rows[:, None], tokens[src_rows], jnp.zeros((), jnp.bfloat16))
        packed_ref = jnp.where(use_rows[:, None], ref_flat[src_rows], jnp.zeros((), jnp.bfloat16)).astype(jnp.float32)
        power = lax.optimization_barrier(jnp.mean(jnp.square(packed_rows.astype(jnp.float32)), axis=1))
        normed = (packed_rows.astype(jnp.float32) * lax.rsqrt(power + EPS)[:, None] * pol_gain[None, :]).astype(jnp.bfloat16)
        values = jnp.dot(normed, pol_weight, preferred_element_type=jnp.float32)
        upstream = cotangent[bin_index].reshape(TP_WAYS * SLOTS, VW).astype(jnp.float32)
        slope = (adv_rows * upstream + pull_rows * (values - packed_ref)).astype(jnp.bfloat16)
        term = lax.dot_general(normed, slope, (((0,), (0,)), ((), ())), preferred_element_type=jnp.float32)
        return (accum + term, values.astype(jnp.bfloat16).reshape(TP_WAYS, SLOTS, VW))
    grad_sum, policy_values = lax.scan(per_bin, jnp.zeros((D, VW), jnp.float32), jnp.arange(BINS, dtype=jnp.int32))
    return (policy_values, grad_sum * factor)
```

```python
import math

import jax
import jax.numpy as jnp
from jax import lax
from jax.experimental import pallas as pl
from jax.experimental.pallas import tpu as pltpu
from jax.sharding import PartitionSpec as P

EPS = 1e-06
BETA = 1.0
MESH = pl.DeviceIdType.MESH
BF = jnp.bfloat16
F32 = jnp.float32

FEAT = 1024
RB = 128
HB = RB // 2
VW = 512
CW = 256
NG = VW // CW
WIDTH = 8192
NDP = 16
SPAN = 16
CHUNK = 64


def kernel(
    x_hbm,
    rw_hbm,
    pw_hbm,
    cot_hbm,
    rg_ref,
    pg_ref,
    len_ref,
    bin_ref,
    adv_ref,
    gap_ref,
    pv_ref,
    gw_ref,
    x,
    xt,
    wr,
    wrs,
    pw,
    wp,
    wps,
    pgc,
    pb,
    ry1,
    ryd,
    ryc,
    ycb,
    qs,
    rz,
    tq,
    z1r,
    sb,
    zr1,
    zrd,
    zrc,
    zcb,
    tref,
    tpol,
    pow_s,
    pow_r,
    cr,
    ss,
    gb,
    dr0,
    hb,
    xr1,
    xrd,
    xrc,
    xcb,
    rb,
    fr,
    pvs,
    pvr,
    loc,
    msend,
    mrecv,
    asend,
    arecv,
    bsend,
    brecv,
    psend,
    precv,
    esend,
    erecv,
    fsend,
    frecv,
    dsend,
    drecv,
    zsend,
):
    d = lax.axis_index("dp")
    t = lax.axis_index("tensor")
    core = d % 2
    xx = (d // 2) % 4
    zh = d // 8
    yy = t % 4
    zl = t // 4
    rel = (xx + 4 - yy) % 4
    odd = rel % 2

    def at(dd, tt):
        return (dd, tt)

    yp = at(d, zl * 4 + (yy + 1) % 4)
    ym = at(d, zl * 4 + (yy + 3) % 4)
    zp = at(d, (1 - zl) * 4 + yy)
    xp = at((zh * 4 + (xx + 1) % 4) * 2 + core, t)
    xm = at((zh * 4 + (xx + 3) % 4) * 2 + core, t)
    cp = at(d + 1 - 2 * core, t)
    zswap = at((1 - zh) * 8 + xx * 2 + core, (1 - zl) * 4 + yy)
    same_z = zh == zl
    diag = rel == 0
    origin = jnp.logical_and(diag, same_z)
    swapper = jnp.logical_and(diag, jnp.logical_not(same_z))
    dfin = (zl * 4 + yy) * 2 + core

    def fin(k):
        return at(dfin, k * 4 + xx)

    def fin_src(s):
        return at((s * 4 + yy) * 2 + core, zh * 4 + xx)

    def fin_self(k):
        return jnp.logical_and(origin, zl == k)

    ld_rw = pltpu.make_async_copy(rw_hbm, wr, loc.at[0])
    ld_x = pltpu.make_async_copy(x_hbm, x, loc.at[1])
    ld_pw = pltpu.make_async_copy(pw_hbm, pw, loc.at[2])
    ld_cot = pltpu.make_async_copy(
        cot_hbm.at[0, 0, pl.ds(pl.multiple_of(d * SPAN, SPAN), SPAN), :], cr.at[d], loc.at[3]
    )
    ld_rw.start()
    ld_x.start()
    ld_pw.start()
    ld_cot.start()

    bar = pltpu.get_barrier_semaphore()

    def greet(dev):
        pl.semaphore_signal(bar, inc=1, device_id=dev, device_id_type=MESH)

    def greet_t(i, c):
        greet(at(d, (t + i) % 8))
        return c

    def greet_d(i, c):
        greet(at((d + i) % NDP, t))
        return c

    lax.fori_loop(1, 8, greet_t, 0)
    lax.fori_loop(1, NDP, greet_d, 0)

    @pl.when(swapper)
    def _():
        greet(zswap)

    for s in range(2):

        @pl.when(jnp.logical_not(jnp.logical_and(origin, zh == s)))
        def _():
            greet(fin_src(s))

    eye = lax.broadcasted_iota(jnp.int32, (RB, RB), 0) == lax.broadcasted_iota(
        jnp.int32, (RB, RB), 1
    )

    def to_col(row):
        return jnp.sum(
            jnp.where(eye, jnp.broadcast_to(row, (RB, RB)), 0.0), axis=1, keepdims=True
        )

    def to_row(col):
        return jnp.sum(
            jnp.where(eye, jnp.broadcast_to(col, (RB, RB)), 0.0), axis=0, keepdims=True
        )

    ld_rw.wait()
    for b in range(8):
        rows = slice(b * RB, (b + 1) * RB)
        gcol = to_col(rg_ref[b : b + 1, :])
        for g in range(NG):
            wrs[g, rows, :] = (wr[rows, g * CW : (g + 1) * CW].astype(F32) * gcol).astype(BF)
        pgc[rows, :] = to_col(pg_ref[t, b : b + 1, :])

    ld_x.wait()

    def products(u, weight):
        def step(i, c):
            rows = pl.ds(pl.multiple_of(i * CW, CW), CW)
            part = jnp.dot(x[rows, :], weight[...], preferred_element_type=F32).astype(BF)
            pb[u, i // 2, (i % 2) * 2] = part[:RB]
            pb[u, i // 2, (i % 2) * 2 + 1] = part[RB:]
            return c

        lax.fori_loop(0, 4, step, 0)

    sent = []
    ids = {}

    def copy(name, src, dst, dev):
        n = ids.setdefault(name, len(ids))
        c = pltpu.make_async_remote_copy(
            src_ref=src,
            dst_ref=dst,
            send_sem=msend.at[n],
            recv_sem=mrecv.at[n],
            device_id=dev,
            device_id_type=MESH,
        )
        c.start()
        sent.append(c)

    def arrived(name, landed):
        n = ids[name]
        pltpu.make_async_remote_copy(
            src_ref=landed,
            dst_ref=landed,
            send_sem=msend.at[n],
            recv_sem=mrecv.at[n],
            device_id=cp,
            device_id_type=MESH,
        ).wait_recv()

    y0, y1, y2, y3 = yy, (yy + 1) % 4, (yy + 2) % 4, (yy + 3) % 4

    def yu_start(u):
        n = u // 2
        copy(("y1", u, 0), pb.at[u, :, y2, 0:HB, :], ry1.at[n, 0], yp)
        copy(("y1", u, 1), pb.at[u, :, y2, HB:RB, :], ry1.at[n, 1], ym)
        copy(("yd", u, 0), pb.at[u, :, y1, HB:RB, :], ryd.at[n, 0], yp)
        copy(("yd", u, 1), pb.at[u, :, y3, 0:HB, :], ryd.at[n, 1], ym)

    def yu_combine(u):
        n = u // 2
        arrived(("y1", u, 0), ry1.at[n, 0])
        ycb[n, 0] = (pb[u, :, y1, 0:HB, :].astype(F32) + ry1[n, 0].astype(F32)).astype(BF)
        copy(("yc", u, 0), ycb.at[n, 0], ryc.at[n, 0], yp)
        arrived(("y1", u, 1), ry1.at[n, 1])
        ycb[n, 1] = (pb[u, :, y3, HB:RB, :].astype(F32) + ry1[n, 1].astype(F32)).astype(BF)
        copy(("yc", u, 1), ycb.at[n, 1], ryc.at[n, 1], ym)

    def yu_cross(u):
        n = u // 2
        for i in range(2):
            arrived(("yd", u, i), ryd.at[n, i])
        for i in range(2):
            arrived(("yc", u, i), ryc.at[n, i])

        def part(zt, lo):
            own = pb[u, zt, y0, lo : lo + HB, :].astype(F32)
            if lo == 0:
                return own + ryc[n, 0, zt].astype(F32) + ryd[n, 1, zt].astype(F32)
            return own + ryd[n, 0, zt].astype(F32) + ryc[n, 1, zt].astype(F32)

        qs[n, 0:HB, :] = part(1 - zl, 0).astype(BF)
        qs[n, HB:RB, :] = part(1 - zl, HB).astype(BF)
        copy(("yz", u), qs.at[n], rz.at[n], zp)
        tq[n, 0:HB, :] = part(zl, 0)
        tq[n, HB:RB, :] = part(zl, HB)

    def yu_finish(u, total, g):
        n = u // 2
        arrived(("yz", u), rz.at[n])
        total[:, g * CW : (g + 1) * CW] = tq[n] + rz[n].astype(F32)

    def zu_start(u):
        n = u // 2
        for o in (2, 1, 3, 0):
            copy(("z1", u, o), pb.at[u, 1 - zl, (yy + o) % 4], z1r.at[n, o], zp)

    def zu_sum(u):
        n = u // 2
        for o in (2, 1, 3):
            arrived(("z1", u, o), z1r.at[n, o])
            sb[n, o] = (pb[u, zl, (yy + o) % 4].astype(F32) + z1r[n, o].astype(F32)).astype(BF)
            if o == 2:
                copy(("zr", u, 0), sb.at[n, 2, 0:HB, :], zr1.at[n, 0], yp)
                copy(("zr", u, 1), sb.at[n, 2, HB:RB, :], zr1.at[n, 1], ym)
            elif o == 1:
                copy(("zd", u, 0), sb.at[n, 1, HB:RB, :], zrd.at[n, 0], yp)
            else:
                copy(("zd", u, 1), sb.at[n, 3, 0:HB, :], zrd.at[n, 1], ym)

    def zu_combine(u):
        n = u // 2
        arrived(("zr", u, 0), zr1.at[n, 0])
        zcb[n, 0] = (sb[n, 1, 0:HB, :].astype(F32) + zr1[n, 0].astype(F32)).astype(BF)
        copy(("zc", u, 0), zcb.at[n, 0], zrc.at[n, 0], yp)
        arrived(("zr", u, 1), zr1.at[n, 1])
        zcb[n, 1] = (sb[n, 3, HB:RB, :].astype(F32) + zr1[n, 1].astype(F32)).astype(BF)
        copy(("zc", u, 1), zcb.at[n, 1], zrc.at[n, 1], ym)

    def zu_finish(u, total, g):
        n = u // 2
        arrived(("z1", u, 0), z1r.at[n, 0])
        for i in range(2):
            arrived(("zd", u, i), zrd.at[n, i])
        for i in range(2):
            arrived(("zc", u, i), zrc.at[n, i])
        cols = slice(g * CW, (g + 1) * CW)
        own = pb[u, zl, y0].astype(F32) + z1r[n, 0].astype(F32)
        total[0:HB, cols] = own[0:HB] + zrc[n, 0].astype(F32) + zrd[n, 1].astype(F32)
        total[HB:RB, cols] = own[HB:RB] + zrd[n, 0].astype(F32) + zrc[n, 1].astype(F32)

    def a_src(q, way):
        return pl.ds(pl.multiple_of(way * 256 + (q % 2) * 128, 128), 128), q // 2

    def a_place(own, q, way):
        return wp.at[
            q // 2,
            pl.ds(pl.multiple_of(own * 512 + way * 256 + (q % 2) * 128, 128), 128),
            :,
        ]

    def a_copy(q, way, dev):
        return pltpu.make_async_remote_copy(
            src_ref=a_place(core, q, way),
            dst_ref=a_place(core, q, way),
            send_sem=asend.at[way * 4 + q],
            recv_sem=arecv.at[way * 4 + q],
            device_id=dev,
            device_id_type=MESH,
        )

    def a_swap(q, way):
        return pltpu.make_async_remote_copy(
            src_ref=pw.at[
                way * 256 + (q % 2) * 128 : way * 256 + (q % 2) * 128 + 128,
                (q // 2) * CW : (q // 2 + 1) * CW,
            ],
            dst_ref=a_place(core, q, way),
            send_sem=zsend.at[way * 4 + q],
            recv_sem=arecv.at[way * 4 + q],
            device_id=zswap,
            device_id_type=MESH,
        )

    def b_copy(own, q, way):
        return pltpu.make_async_remote_copy(
            src_ref=a_place(own, q, way),
            dst_ref=a_place(own, q, way),
            send_sem=bsend.at[way * 4 + q],
            recv_sem=brecv.at[way * 4 + q],
            device_id=cp,
            device_id_type=MESH,
        )

    def a_order(i):
        q = odd * (i % 4) + (1 - odd) * (i // 2)
        way = odd * ((i // 4 + rel // 2) % 2) + (1 - odd) * (i % 2)
        return q, way

    def a_next(way):
        return at((zh * 4 + (xx + 1 + 2 * way) % 4) * 2 + core, t)

    def a_forwards(way):
        return rel != 3 - 2 * way

    def a_step(i):
        q, way = a_order(i)

        @pl.when(jnp.logical_not(origin))
        def _():
            a_copy(q, way, xp).wait_recv()

        @pl.when(a_forwards(way))
        def _():
            a_copy(q, way, a_next(way)).start()

        b_copy(core, q, way).start()

    products(0, wrs.at[0])
    products(1, wrs.at[1])

    ld_pw.wait()

    @pl.when(origin)
    def _():
        for g in range(NG):
            wp[g, pl.ds(pl.multiple_of(core * 512, 512), 512), :] = pw[:, g * CW : (g + 1) * CW]

    pl.semaphore_wait(
        bar,
        22
        + jnp.where(swapper, 1, 0)
        + jnp.where(fin_self(0), 0, 1)
        + jnp.where(fin_self(1), 0, 1),
    )

    @pl.when(swapper)
    def _():
        for q in range(4):
            for way in range(2):
                a_swap(q, way).start()

    @pl.when(origin)
    def _():
        for i in range(8):
            a_step(i)

    yu_start(0)
    zu_start(1)

    def squares(b, c):
        rows = pl.ds(pl.multiple_of(b * RB, RB), RB)
        xb = x[rows, :].astype(F32)
        part = jnp.sum(xb * xb, axis=1, keepdims=True)
        pow_s[b] = jnp.broadcast_to(to_row(part), (8, RB))
        return c

    lax.fori_loop(0, 8, squares, 0)
    pow_r[t] = pow_s[t]

    def p_copy(peer):
        return pltpu.make_async_remote_copy(
            src_ref=pow_s.at[peer],
            dst_ref=pow_r.at[t],
            send_sem=psend.at[peer],
            recv_sem=precv.at[t],
            device_id=at(d, peer),
            device_id_type=MESH,
        )

    def p_start(i, c):
        p_copy((t + i) % 8).start()
        return c

    lax.fori_loop(1, 8, p_start, 0)

    def a_step_others(i):
        @pl.when(jnp.logical_not(origin))
        def _():
            a_step(i)

    a_step_others(0)
    yu_combine(0)
    a_step_others(1)
    zu_sum(1)
    a_step_others(2)
    a_step_others(3)
    zu_combine(1)
    a_step_others(4)
    a_step_others(5)
    yu_cross(0)

    def e_copy(peer):
        return pltpu.make_async_remote_copy(
            src_ref=cot_hbm.at[0, 0, pl.ds(pl.multiple_of(peer * SPAN, SPAN), SPAN), :],
            dst_ref=cr.at[d],
            send_sem=esend.at[peer],
            recv_sem=erecv.at[d],
            device_id=at(peer, t),
            device_id_type=MESH,
        )

    def e_start(i, c):
        e_copy((d + i) % NDP).start()
        return c

    def policy(g):
        for way in range(2):
            for q in (2 * g, 2 * g + 1):
                b_copy(1 - core, q, way).wait_recv()
        for b in range(8):
            rows = slice(b * RB, (b + 1) * RB)
            wps[g, rows, :] = (wp[g, rows, :].astype(F32) * pgc[rows, :]).astype(BF)
        products(2 + g, wps.at[g])

    policy(0)
    yu_start(2)
    a_step_others(6)
    a_step_others(7)
    lax.fori_loop(1, NDP, e_start, 0)
    policy(1)
    zu_start(3)
    zu_finish(1, tref, 1)
    yu_finish(0, tref, 0)

    def turn(i, c):
        cols = pl.ds(pl.multiple_of(i * CW, CW), CW)
        xt[cols, :] = x[:, cols].T
        return c

    lax.fori_loop(0, 4, turn, 0)
    yu_combine(2)

    row = lax.broadcasted_iota(jnp.int32, (RB, 1), 0)
    slot = jnp.zeros((RB, 1), jnp.int32)
    length = jnp.ones((RB, 1), F32)
    advantage = jnp.zeros((RB, 1), F32)
    start = jnp.int32(0)
    for s in range(16):
        n = len_ref[0, 0, s]
        inside = jnp.logical_and(row >= start, row < start + n)
        slot = jnp.where(inside, row - start + bin_ref[0, 0, s] * SPAN, slot)
        length = jnp.where(inside, n.astype(F32), length)
        advantage = jnp.where(inside, adv_ref[0, 0, s], advantage)
        start = start + n
    importance = jnp.minimum(jnp.exp(to_col(gap_ref[...])), 2.0)
    coef_adv = (advantage * importance / length).astype(BF).astype(F32)
    coef_pull = (BETA / length).astype(BF).astype(F32)
    pick = (
        jnp.broadcast_to(slot, (RB, NDP * SPAN))
        == lax.broadcasted_iota(jnp.int32, (RB, NDP * SPAN), 1)
    ).astype(BF)
    slot_row = to_row(slot.astype(F32))
    place = (
        lax.broadcasted_iota(jnp.int32, (NDP * SPAN, RB), 0).astype(F32)
        == jnp.broadcast_to(slot_row, (NDP * SPAN, RB))
    ).astype(BF)

    def p_wait(i, c):
        p = (t + i) % 8
        pltpu.make_async_remote_copy(
            src_ref=pow_r.at[p],
            dst_ref=pow_r.at[p],
            send_sem=psend.at[p],
            recv_sem=precv.at[p],
            device_id=at(d, p),
            device_id_type=MESH,
        ).wait_recv()
        return c

    lax.fori_loop(1, 8, p_wait, 0)
    power = pow_r[0]
    for k in range(1, 8):
        power = power + pow_r[k]
    scale = to_col(lax.rsqrt(power[0:1, :] * (1.0 / WIDTH) + EPS))

    zu_sum(3)
    yu_cross(2)
    zu_combine(3)

    ld_cot.wait()

    def e_wait(i, c):
        p = (d + i) % NDP
        pltpu.make_async_remote_copy(
            src_ref=cr.at[p],
            dst_ref=cr.at[p],
            send_sem=esend.at[p],
            recv_sem=erecv.at[p],
            device_id=at(p, t),
            device_id_type=MESH,
        ).wait_recv()
        return c

    lax.fori_loop(1, NDP, e_wait, 0)

    def slopes(g):
        cols = slice(g * CW, (g + 1) * CW)
        upstream = jnp.dot(
            pick, cr[:, :, cols].reshape(NDP * SPAN, CW), preferred_element_type=F32
        )
        values = tpol[:, cols] * scale
        ref_values = (tref[:, cols] * scale).astype(BF).astype(F32)
        slope = coef_adv * upstream + coef_pull * (values - ref_values)
        ss[g, zl, y0] = (slope * scale).astype(BF)
        mine = ss.at[g, zl, y0]
        copy(("cz", g), mine, mine, zp)
        copy(("cp", g), mine, mine, yp)
        copy(("cm", g), mine, mine, ym)
        out = jnp.dot(place, values.astype(BF), preferred_element_type=F32).astype(BF)
        pvs[:, :, cols] = out.reshape(NDP, SPAN, CW)

    def spread(g):
        oz = 1 - zl
        arrived(("cz", g), ss.at[g, oz, y0])
        block = ss.at[g, oz, y0]
        copy(("czp", g), block, block, yp)
        copy(("czm", g), block, block, ym)
        arrived(("cp", g), ss.at[g, zl, y3])
        half = ss.at[g, zl, y3, 0:HB, :]
        copy(("chp", g), half, half, yp)
        arrived(("cm", g), ss.at[g, zl, y1])
        half = ss.at[g, zl, y1, HB:RB, :]
        copy(("chm", g), half, half, ym)

    def spread_far(g):
        arrived(("chp", g), ss.at[g, zl, y2, 0:HB, :])
        arrived(("chm", g), ss.at[g, zl, y2, HB:RB, :])
        block = ss.at[g, zl, y2]
        copy(("czz", g), block, block, zp)

    def spread_end(g):
        oz = 1 - zl
        arrived(("czp", g), ss.at[g, oz, y3])
        arrived(("czm", g), ss.at[g, oz, y1])
        arrived(("czz", g), ss.at[g, oz, y2])

    factor = 1.0 / math.sqrt(2048.0)

    def gradient(g, half):
        def step(i, c):
            base = pl.multiple_of((half * 2 + i) * CW, CW)
            rows = pl.ds(base, CW)
            part = jnp.dot(
                xt[rows, :], ss[g].reshape(FEAT, CW), preferred_element_type=F32
            )
            part = (part * (pgc[rows, :] * factor)).astype(BF)
            gb[g, half, pl.ds(pl.multiple_of(i * 4, 4), 4)] = part.reshape(4, CHUNK, CW)
            return c

        lax.fori_loop(0, 2, step, 0)

    def reduce_core(g):
        gradient(g, 1 - core)
        copy(("d0", g), gb.at[g, 1 - core], dr0.at[g], cp)
        gradient(g, core)

    x0, x1, x2, x3 = xx, (xx + 1) % 4, (xx + 2) % 4, (xx + 3) % 4

    def reduce_x(g):
        arrived(("d0", g), dr0.at[g])
        hb[g] = (gb[g, core].astype(F32) + dr0[g].astype(F32)).astype(BF)
        copy(("x1", g, 0), hb.at[g, x2], xr1.at[g, 0], xp)
        copy(("x1", g, 1), hb.at[g, 4 + x2], xr1.at[g, 1], xm)
        copy(("xd", g, 0), hb.at[g, 4 + x1], xrd.at[g, 0], xp)
        copy(("xd", g, 1), hb.at[g, x3], xrd.at[g, 1], xm)

    def combine_x(g):
        arrived(("x1", g, 0), xr1.at[g, 0])
        xcb[g, 0] = (hb[g, x1].astype(F32) + xr1[g, 0].astype(F32)).astype(BF)
        copy(("xc", g, 0), xcb.at[g, 0], xrc.at[g, 0], xp)
        arrived(("x1", g, 1), xr1.at[g, 1])
        xcb[g, 1] = (hb[g, 4 + x3].astype(F32) + xr1[g, 1].astype(F32)).astype(BF)
        copy(("xc", g, 1), xcb.at[g, 1], xrc.at[g, 1], xm)

    def d_copy(g, k):
        return pltpu.make_async_remote_copy(
            src_ref=rb.at[g, k],
            dst_ref=fr.at[g, zh],
            send_sem=dsend.at[g * 2 + k],
            recv_sem=drecv.at[g * 2 + zh],
            device_id=fin(k),
            device_id_type=MESH,
        )

    def to_owner(g):
        for i in range(2):
            arrived(("xd", g, i), xrd.at[g, i])
        for i in range(2):
            arrived(("xc", g, i), xrc.at[g, i])
        rb[g, 0] = (
            hb[g, x0].astype(F32) + xrc[g, 0].astype(F32) + xrd[g, 1].astype(F32)
        ).astype(BF)
        rb[g, 1] = (
            hb[g, 4 + x0].astype(F32) + xrd[g, 0].astype(F32) + xrc[g, 1].astype(F32)
        ).astype(BF)
        for k in range(2):

            @pl.when(fin_self(k))
            def _():
                fr[g, zh] = rb[g, k]

            @pl.when(jnp.logical_not(fin_self(k)))
            def _():
                d_copy(g, k).start()

    def finish(g):
        for s in range(2):

            @pl.when(jnp.logical_not(jnp.logical_and(origin, zh == s)))
            def _():
                pltpu.make_async_remote_copy(
                    src_ref=fr.at[g, s],
                    dst_ref=fr.at[g, s],
                    send_sem=dsend.at[g * 2],
                    recv_sem=drecv.at[g * 2 + s],
                    device_id=cp,
                    device_id_type=MESH,
                ).wait_recv()

        gw_ref[:, g * CW : (g + 1) * CW] = fr[g, 0].astype(F32) + fr[g, 1].astype(F32)

    def f_copy(peer):
        return pltpu.make_async_remote_copy(
            src_ref=pvs.at[peer],
            dst_ref=pvr.at[d],
            send_sem=fsend.at[peer],
            recv_sem=frecv.at[d],
            device_id=at(peer, t),
            device_id_type=MESH,
        )

    def f_start(i, c):
        f_copy((d + i) % NDP).start()
        return c

    def f_wait(i, c):
        p = (d + i) % NDP
        pltpu.make_async_remote_copy(
            src_ref=pvr.at[p],
            dst_ref=pvr.at[p],
            send_sem=fsend.at[p],
            recv_sem=frecv.at[p],
            device_id=at(p, t),
            device_id_type=MESH,
        ).wait_recv()
        return c

    yu_finish(2, tpol, 0)
    slopes(0)
    zu_finish(3, tpol, 1)
    slopes(1)
    spread(0)
    pvr[d] = pvs[d]
    lax.fori_loop(1, NDP, f_start, 0)
    spread(1)
    spread_far(0)
    spread_far(1)
    spread_end(0)
    reduce_core(0)
    reduce_x(0)
    spread_end(1)
    reduce_core(1)
    combine_x(0)
    reduce_x(1)
    to_owner(0)
    combine_x(1)
    lax.fori_loop(1, NDP, f_wait, 0)
    pv_ref[0, 0] = pvr[...].reshape(NDP * SPAN, VW)
    to_owner(1)
    finish(0)
    finish(1)

    for c in sent:
        c.wait_send()

    @pl.when(swapper)
    def _():
        for q in range(4):
            for way in range(2):
                a_swap(q, way).wait_send()

    for way in range(2):

        @pl.when(a_forwards(way))
        def _():
            for q in range(4):
                a_copy(q, way, a_next(way)).wait_send()

        for q in range(4):
            b_copy(core, q, way).wait_send()

    def p_done(i, c):
        p_copy((t + i) % 8).wait_send()
        return c

    def ef_done(i, c):
        e_copy((d + i) % NDP).wait_send()
        f_copy((d + i) % NDP).wait_send()
        return c

    lax.fori_loop(1, 8, p_done, 0)
    lax.fori_loop(1, NDP, ef_done, 0)
    for g in range(NG):
        for k in range(2):

            @pl.when(jnp.logical_not(fin_self(k)))
            def _():
                d_copy(g, k).wait_send()


def on_device(
    tokens,
    ref_gain,
    ref_weight,
    pol_gain,
    pol_weight,
    lengths,
    bins,
    advantage,
    logprob_gap,
    cotangent,
):
    any_spec = pl.BlockSpec(memory_space=pl.ANY)
    vmem = pl.BlockSpec(memory_space=pltpu.VMEM)
    smem = pl.BlockSpec(memory_space=pltpu.SMEM)
    dma = pltpu.SemaphoreType.DMA

    def buf(*shape, dtype=BF):
        return pltpu.VMEM(shape, dtype)

    return pl.pallas_call(
        kernel,
        out_shape=(
            jax.ShapeDtypeStruct(cotangent.shape, BF),
            jax.ShapeDtypeStruct((CHUNK, VW), F32),
        ),
        in_specs=[any_spec] * 4 + [vmem, vmem, smem, smem, smem, vmem],
        out_specs=(vmem, vmem),
        scratch_shapes=[
            buf(1024, FEAT),
            buf(FEAT, 1024),
            buf(FEAT, VW),
            buf(NG, FEAT, CW),
            buf(512, VW),
            buf(NG, FEAT, CW),
            buf(NG, FEAT, CW),
            buf(FEAT, 1, dtype=F32),
            buf(4, 2, 4, RB, CW),
            buf(2, 2, 2, HB, CW),
            buf(2, 2, 2, HB, CW),
            buf(2, 2, 2, HB, CW),
            buf(2, 2, 2, HB, CW),
            buf(2, RB, CW),
            buf(2, RB, CW),
            buf(2, RB, CW, dtype=F32),
            buf(2, 4, RB, CW),
            buf(2, 4, RB, CW),
            buf(2, 2, HB, CW),
            buf(2, 2, HB, CW),
            buf(2, 2, HB, CW),
            buf(2, 2, HB, CW),
            buf(RB, VW, dtype=F32),
            buf(RB, VW, dtype=F32),
            buf(8, 8, RB, dtype=F32),
            buf(8, 8, RB, dtype=F32),
            buf(NDP, SPAN, VW),
            buf(NG, 2, 4, RB, CW),
            buf(NG, 2, 8, CHUNK, CW),
            buf(NG, 8, CHUNK, CW),
            buf(NG, 8, CHUNK, CW),
            buf(NG, 2, CHUNK, CW),
            buf(NG, 2, CHUNK, CW),
            buf(NG, 2, CHUNK, CW),
            buf(NG, 2, CHUNK, CW),
            buf(NG, 2, CHUNK, CW),
            buf(NG, 2, CHUNK, CW),
            buf(NDP, SPAN, VW),
            buf(NDP, SPAN, VW),
            dma((4,)),
            dma((64,)),
            dma((64,)),
            dma((8,)),
            dma((8,)),
            dma((8,)),
            dma((8,)),
            dma((8,)),
            dma((8,)),
            dma((NDP,)),
            dma((NDP,)),
            dma((NDP,)),
            dma((NDP,)),
            dma((4,)),
            dma((4,)),
            dma((8,)),
        ],
        compiler_params=pltpu.CompilerParams(collective_id=0, has_side_effects=True),
    )(
        tokens,
        ref_weight,
        pol_weight,
        cotangent,
        ref_gain.reshape(8, RB),
        pol_gain.reshape(8, 8, RB),
        lengths,
        bins,
        advantage,
        logprob_gap.reshape(1, RB),
    )


def solution(mesh):
    in_specs = (
        P("dp", "tensor"),
        P("tensor"),
        P("tensor", None),
        P(),
        P("dp", None),
        P("dp", "tensor", None),
        P("dp", "tensor", None),
        P("dp", "tensor", None),
        P(("dp", "tensor")),
        P("dp", "tensor", None, None),
    )
    out_specs = (P("dp", "tensor", None, None), P(("dp", "tensor"), None))
    return jax.shard_map(
        on_device, mesh=mesh, in_specs=in_specs, out_specs=out_specs, check_vma=False
    )
```

```python
import math

import jax
import jax.numpy as jnp
from jax import lax
from jax.experimental import pallas as pl
from jax.experimental.pallas import tpu as pltpu
from jax.sharding import PartitionSpec as P

EPS = 1e-06
BETA = 1.0
MESH = pl.DeviceIdType.MESH
BF = jnp.bfloat16
F32 = jnp.float32

FEAT = 1024
RB = 128
HB = RB // 2
VW = 512
CW = 256
NG = VW // CW
WIDTH = 8192
NDP = 16
SPAN = 16
AP = 64
MODES = "yzee"
CHUNK = 64


def kernel(
    x_hbm,
    rw_hbm,
    pw_hbm,
    cot_hbm,
    rg_ref,
    pg_ref,
    len_ref,
    bin_ref,
    adv_ref,
    gap_ref,
    pv_ref,
    gw_ref,
    x,
    xt,
    wr,
    wrs,
    pw,
    wp,
    wps,
    pgc,
    pb,
    ry1,
    ryd,
    ryc,
    re,
    ycb,
    qs,
    rz,
    tq,
    z1r,
    sb,
    zr1,
    zrd,
    zrc,
    zcb,
    tref,
    tpol,
    pow_s,
    pow_r,
    cr,
    ss,
    gb,
    dr0,
    hb,
    xr,
    rb,
    fr,
    pvs,
    pvr,
    loc,
    msend,
    mrecv,
    asend,
    arecv,
    psend,
    precv,
    esend,
    erecv,
    fsend,
    frecv,
    dsend,
    drecv,
):
    d = lax.axis_index("dp")
    t = lax.axis_index("tensor")
    core = d % 2
    xx = (d // 2) % 4
    zh = d // 8
    yy = t % 4
    zl = t // 4

    def at(dd, tt):
        return (dd, tt)

    yp = at(d, zl * 4 + (yy + 1) % 4)
    ym = at(d, zl * 4 + (yy + 3) % 4)
    yf = at(d, zl * 4 + (yy + 2) % 4)
    zp = at(d, (1 - zl) * 4 + yy)
    xp = at((zh * 4 + (xx + 1) % 4) * 2 + core, t)
    xm = at((zh * 4 + (xx + 3) % 4) * 2 + core, t)
    xf = at((zh * 4 + (xx + 2) % 4) * 2 + core, t)
    cp = at(d + 1 - 2 * core, t)
    same_z = zh == zl
    origin = jnp.logical_and(xx == yy, same_z)
    dfin = (zl * 4 + yy) * 2 + core

    def fin(k):
        return at(dfin, k * 4 + xx)

    def fin_src(s):
        return at((s * 4 + yy) * 2 + core, zh * 4 + xx)

    def fin_self(k):
        return jnp.logical_and(origin, zl == k)

    ld_rw = pltpu.make_async_copy(rw_hbm, wr, loc.at[0])
    ld_x = pltpu.make_async_copy(x_hbm, x, loc.at[1])
    ld_pw = pltpu.make_async_copy(pw_hbm, pw, loc.at[2])
    ld_cot = pltpu.make_async_copy(
        cot_hbm.at[0, 0, pl.ds(pl.multiple_of(d * SPAN, SPAN), SPAN), :], cr.at[d], loc.at[3]
    )
    ld_rw.start()
    ld_x.start()
    ld_pw.start()
    ld_cot.start()

    bar = pltpu.get_barrier_semaphore()

    def greet(dev):
        pl.semaphore_signal(bar, inc=1, device_id=dev, device_id_type=MESH)

    def greet_t(i, c):
        greet(at(d, (t + i) % 8))
        return c

    def greet_d(i, c):
        greet(at((d + i) % NDP, t))
        return c

    lax.fori_loop(1, 8, greet_t, 0)
    lax.fori_loop(1, NDP, greet_d, 0)

    def greet_w(i, c):
        @pl.when(jnp.logical_or(d // 2 != t, i != t))
        def _():
            greet(at(2 * t + core, i))

        return c

    lax.fori_loop(0, 8, greet_w, 0)

    for s in range(2):

        @pl.when(jnp.logical_not(jnp.logical_and(origin, zh == s)))
        def _():
            greet(fin_src(s))

    eye = lax.broadcasted_iota(jnp.int32, (RB, RB), 0) == lax.broadcasted_iota(
        jnp.int32, (RB, RB), 1
    )

    def to_col(row):
        return jnp.sum(
            jnp.where(eye, jnp.broadcast_to(row, (RB, RB)), 0.0), axis=1, keepdims=True
        )

    def to_row(col):
        return jnp.sum(
            jnp.where(eye, jnp.broadcast_to(col, (RB, RB)), 0.0), axis=0, keepdims=True
        )

    ld_rw.wait()
    for b in range(8):
        rows = slice(b * RB, (b + 1) * RB)
        gcol = to_col(rg_ref[b : b + 1, :])
        for g in range(NG):
            wrs[g, rows, :] = (wr[rows, g * CW : (g + 1) * CW].astype(F32) * gcol).astype(BF)
        pgc[rows, :] = to_col(pg_ref[t, b : b + 1, :])

    ld_x.wait()

    def products(u, weight):
        def step(i, c):
            rows = pl.ds(pl.multiple_of(i * CW, CW), CW)
            part = jnp.dot(x[rows, :], weight[...], preferred_element_type=F32).astype(BF)
            pb[u, i // 2, (i % 2) * 2] = part[:RB]
            pb[u, i // 2, (i % 2) * 2 + 1] = part[RB:]
            return c

        lax.fori_loop(0, 4, step, 0)

    sent = []
    ids = {}

    def copy(name, src, dst, dev):
        n = ids.setdefault(name, len(ids))
        c = pltpu.make_async_remote_copy(
            src_ref=src,
            dst_ref=dst,
            send_sem=msend.at[n],
            recv_sem=mrecv.at[n],
            device_id=dev,
            device_id_type=MESH,
        )
        c.start()
        sent.append(c)

    def arrived(name, landed):
        n = ids[name]
        pltpu.make_async_remote_copy(
            src_ref=landed,
            dst_ref=landed,
            send_sem=msend.at[n],
            recv_sem=mrecv.at[n],
            device_id=cp,
            device_id_type=MESH,
        ).wait_recv()

    y0, y1, y2, y3 = yy, (yy + 1) % 4, (yy + 2) % 4, (yy + 3) % 4

    def start_y(u):
        n = u
        copy(("y1", u, 0), pb.at[u, :, y2, 0:HB, :], ry1.at[n, 0], yp)
        copy(("y1", u, 1), pb.at[u, :, y2, HB:RB, :], ry1.at[n, 1], ym)
        copy(("yd", u, 0), pb.at[u, :, y1, HB:RB, :], ryd.at[n, 0], yp)
        copy(("yd", u, 1), pb.at[u, :, y3, 0:HB, :], ryd.at[n, 1], ym)

    def combine_y(u):
        n = u
        arrived(("y1", u, 0), ry1.at[n, 0])
        ycb[n, 0] = (pb[u, :, y1, 0:HB, :].astype(F32) + ry1[n, 0].astype(F32)).astype(BF)
        copy(("yc", u, 0), ycb.at[n, 0], ryc.at[n, 0], yp)
        arrived(("y1", u, 1), ry1.at[n, 1])
        ycb[n, 1] = (pb[u, :, y3, HB:RB, :].astype(F32) + ry1[n, 1].astype(F32)).astype(BF)
        copy(("yc", u, 1), ycb.at[n, 1], ryc.at[n, 1], ym)

    def cross_y(u):
        n = u
        for i in range(2):
            arrived(("yd", u, i), ryd.at[n, i])
        for i in range(2):
            arrived(("yc", u, i), ryc.at[n, i])

        def part(zt, lo):
            own = pb[u, zt, y0, lo : lo + HB, :].astype(F32)
            if lo == 0:
                return own + ryc[n, 0, zt].astype(F32) + ryd[n, 1, zt].astype(F32)
            return own + ryd[n, 0, zt].astype(F32) + ryc[n, 1, zt].astype(F32)

        qs[n, 0:HB, :] = part(1 - zl, 0).astype(BF)
        qs[n, HB:RB, :] = part(1 - zl, HB).astype(BF)
        copy(("yz", u), qs.at[n], rz.at[n], zp)
        tq[n, 0:HB, :] = part(zl, 0)
        tq[n, HB:RB, :] = part(zl, HB)

    def finish_y(u, total, g):
        n = u
        arrived(("yz", u), rz.at[n])
        total[:, g * CW : (g + 1) * CW] = tq[n] + rz[n].astype(F32)

    def start_z(u):
        n = u
        for o in (2, 1, 3, 0):
            copy(("z1", u, o), pb.at[u, 1 - zl, (yy + o) % 4], z1r.at[n, o], zp)

    def sum_z(u):
        n = u
        for o in (2, 1, 3):
            arrived(("z1", u, o), z1r.at[n, o])
            sb[n, o] = (pb[u, zl, (yy + o) % 4].astype(F32) + z1r[n, o].astype(F32)).astype(BF)
            if o == 2:
                copy(("zr", u, 0), sb.at[n, 2, 0:HB, :], zr1.at[n, 0], yp)
                copy(("zr", u, 1), sb.at[n, 2, HB:RB, :], zr1.at[n, 1], ym)
            elif o == 1:
                copy(("zd", u, 0), sb.at[n, 1, HB:RB, :], zrd.at[n, 0], yp)
            else:
                copy(("zd", u, 1), sb.at[n, 3, 0:HB, :], zrd.at[n, 1], ym)

    def combine_z(u):
        n = u
        arrived(("zr", u, 0), zr1.at[n, 0])
        zcb[n, 0] = (sb[n, 1, 0:HB, :].astype(F32) + zr1[n, 0].astype(F32)).astype(BF)
        copy(("zc", u, 0), zcb.at[n, 0], zrc.at[n, 0], yp)
        arrived(("zr", u, 1), zr1.at[n, 1])
        zcb[n, 1] = (sb[n, 3, HB:RB, :].astype(F32) + zr1[n, 1].astype(F32)).astype(BF)
        copy(("zc", u, 1), zcb.at[n, 1], zrc.at[n, 1], ym)

    def finish_z(u, total, g):
        n = u
        arrived(("z1", u, 0), z1r.at[n, 0])
        for i in range(2):
            arrived(("zd", u, i), zrd.at[n, i])
        for i in range(2):
            arrived(("zc", u, i), zrc.at[n, i])
        cols = slice(g * CW, (g + 1) * CW)
        own = pb[u, zl, y0].astype(F32) + z1r[n, 0].astype(F32)
        total[0:HB, cols] = own[0:HB] + zrc[n, 0].astype(F32) + zrd[n, 1].astype(F32)
        total[HB:RB, cols] = own[HB:RB] + zrd[n, 0].astype(F32) + zrc[n, 1].astype(F32)

    def start_e(u):
        copy(("e", u, 2), pb.at[u, :, y2], re.at[u, 2], yf)
        copy(("e", u, 0), pb.at[u, :, y1], re.at[u, 0], yp)
        copy(("e", u, 1), pb.at[u, :, y3], re.at[u, 1], ym)

    def none(u):
        pass

    def cross_e(u):
        for i in range(3):
            arrived(("e", u, i), re.at[u, i])

        def part(zt):
            whole = pb[u, zt, y0].astype(F32)
            for i in range(3):
                whole = whole + re[u, i, zt].astype(F32)
            return whole

        qs[u] = part(1 - zl).astype(BF)
        copy(("yz", u), qs.at[u], rz.at[u], zp)
        tq[u] = part(zl)

    def unit(u):
        if MODES[u] == "e":
            return start_e, none, cross_e, finish_y
        return (start_y, combine_y, cross_y, finish_y) if MODES[u] == "y" else (start_z, sum_z, combine_z, finish_z)

    def start(u):
        unit(u)[0](u)

    def second(u):
        unit(u)[1](u)

    def third(u):
        unit(u)[2](u)

    def finish_unit(u):
        unit(u)[3](u, (tref, tref, tpol, tpol)[u], u % 2)

    def w_copy(g, i):
        rank = (d // 2 + t + i) % 8
        return pltpu.make_async_remote_copy(
            src_ref=pw.at[
                pl.ds(pl.multiple_of(t * AP, AP), AP), g * CW : (g + 1) * CW
            ],
            dst_ref=wp.at[g, pl.ds(pl.multiple_of(core * 512 + t * AP, AP), AP), :],
            send_sem=asend.at[g * 8 + rank],
            recv_sem=arecv.at[g * 8 + t],
            device_id=at(rank * 2 + core, d // 2),
            device_id_type=MESH,
        )

    def w_remote(i):
        return jnp.logical_or(d // 2 != t, (d // 2 + t + i) % 8 != d // 2)

    def w_start(g):
        def step(i, c):
            @pl.when(w_remote(i))
            def _():
                w_copy(g, i).start()

            return c

        lax.fori_loop(0, 8, step, 0)

    def w_sent(g):
        def step(i, c):
            @pl.when(w_remote(i))
            def _():
                w_copy(g, i).wait_send()

            return c

        lax.fori_loop(0, 8, step, 0)

    def w_share(g):
        def step(i, c):
            part = wp.at[g, pl.ds(pl.multiple_of(core * 512 + i * AP, AP), AP), :]

            @pl.when(jnp.logical_or(d // 2 != t, i != t))
            def _():
                pltpu.make_async_remote_copy(
                    src_ref=part,
                    dst_ref=part,
                    send_sem=asend.at[g * 8 + i],
                    recv_sem=arecv.at[g * 8 + i],
                    device_id=cp,
                    device_id_type=MESH,
                ).wait_recv()

            return c

        lax.fori_loop(0, 8, step, 0)
        mine = wp.at[g, pl.ds(pl.multiple_of(core * 512, 512), 512), :]
        copy(("w", g), mine, mine, cp)

    products(0, wrs.at[0])
    products(1, wrs.at[1])

    ld_pw.wait()

    @pl.when(d // 2 == t)
    def _():
        for g in range(NG):
            wp[g, pl.ds(pl.multiple_of(core * 512 + t * AP, AP), AP), :] = pw[
                pl.ds(pl.multiple_of(t * AP, AP), AP), g * CW : (g + 1) * CW
            ]

    pl.semaphore_wait(
        bar,
        30
        - jnp.where(d // 2 == t, 1, 0)
        + jnp.where(fin_self(0), 0, 1)
        + jnp.where(fin_self(1), 0, 1),
    )


    w_start(0)
    start(0)
    w_start(1)
    start(1)

    def squares(b, c):
        rows = pl.ds(pl.multiple_of(b * RB, RB), RB)
        xb = x[rows, :].astype(F32)
        part = jnp.sum(xb * xb, axis=1, keepdims=True)
        pow_s[b] = jnp.broadcast_to(to_row(part), (8, RB))
        return c

    lax.fori_loop(0, 8, squares, 0)
    pow_r[t] = pow_s[t]

    def p_copy(peer):
        return pltpu.make_async_remote_copy(
            src_ref=pow_s.at[peer],
            dst_ref=pow_r.at[t],
            send_sem=psend.at[peer],
            recv_sem=precv.at[t],
            device_id=at(d, peer),
            device_id_type=MESH,
        )

    def p_start(i, c):
        p_copy((t + i) % 8).start()
        return c

    lax.fori_loop(1, 8, p_start, 0)


    def e_copy(peer):
        return pltpu.make_async_remote_copy(
            src_ref=cot_hbm.at[0, 0, pl.ds(pl.multiple_of(peer * SPAN, SPAN), SPAN), :],
            dst_ref=cr.at[d],
            send_sem=esend.at[peer],
            recv_sem=erecv.at[d],
            device_id=at(peer, t),
            device_id_type=MESH,
        )

    def e_start(i, c):
        e_copy((d + i) % NDP).start()
        return c

    def policy(g):
        arrived(("w", g), wp.at[g, pl.ds(pl.multiple_of((1 - core) * 512, 512), 512), :])
        for b in range(8):
            rows = slice(b * RB, (b + 1) * RB)
            wps[g, rows, :] = (wp[g, rows, :].astype(F32) * pgc[rows, :]).astype(BF)
        products(2 + g, wps.at[g])

    def slopes(g):
        cols = slice(g * CW, (g + 1) * CW)
        upstream = jnp.dot(
            pick, cr[:, :, cols].reshape(NDP * SPAN, CW), preferred_element_type=F32
        )
        values = tpol[:, cols] * scale
        ref_values = (tref[:, cols] * scale).astype(BF).astype(F32)
        slope = coef_adv * upstream + coef_pull * (values - ref_values)
        ss[g, zl, y0] = (slope * scale).astype(BF)
        mine = ss.at[g, zl, y0]
        copy(("cf", g), mine, mine, yf)
        copy(("cz", g), mine, mine, zp)
        copy(("cp", g), mine, mine, yp)
        copy(("cm", g), mine, mine, ym)
        out = jnp.dot(place, values.astype(BF), preferred_element_type=F32).astype(BF)
        pvs[:, :, cols] = out.reshape(NDP, SPAN, CW)

    def spread(g):
        oz = 1 - zl
        arrived(("cz", g), ss.at[g, oz, y0])
        block = ss.at[g, oz, y0]
        copy(("czp", g), block, block, yp)
        copy(("czm", g), block, block, ym)

    def spread_far(g):
        block = ss.at[g, zl, y2]
        arrived(("cf", g), block)
        copy(("czz", g), block, block, zp)

    def spread_end(g):
        oz = 1 - zl
        arrived(("cp", g), ss.at[g, zl, y3])
        arrived(("cm", g), ss.at[g, zl, y1])
        arrived(("czp", g), ss.at[g, oz, y3])
        arrived(("czm", g), ss.at[g, oz, y1])
        arrived(("czz", g), ss.at[g, oz, y2])

    factor = 1.0 / math.sqrt(2048.0)

    def gradient(g, half):
        def step(i, c):
            base = pl.multiple_of((half * 2 + i) * CW, CW)
            rows = pl.ds(base, CW)
            part = jnp.dot(
                xt[rows, :], ss[g].reshape(FEAT, CW), preferred_element_type=F32
            )
            part = (part * (pgc[rows, :] * factor)).astype(BF)
            gb[g, half, pl.ds(pl.multiple_of(i * 4, 4), 4)] = part.reshape(4, CHUNK, CW)
            return c

        lax.fori_loop(0, 2, step, 0)

    def reduce_core(g):
        gradient(g, 1 - core)
        copy(("d0", g), gb.at[g, 1 - core], dr0.at[g], cp)
        gradient(g, core)

    x0, x1, x2, x3 = xx, (xx + 1) % 4, (xx + 2) % 4, (xx + 3) % 4

    def reduce_x(g):
        arrived(("d0", g), dr0.at[g])
        hb[g] = (gb[g, core].astype(F32) + dr0[g].astype(F32)).astype(BF)
        for i, (quarter, dev) in enumerate(((x2, xf), (x1, xp), (x3, xm))):
            for k in range(2):
                copy(("x", g, i, k), hb.at[g, 4 * k + quarter], xr.at[g, i, k], dev)

    def d_copy(g, k):
        return pltpu.make_async_remote_copy(
            src_ref=rb.at[g, k],
            dst_ref=fr.at[g, zh],
            send_sem=dsend.at[g * 2 + k],
            recv_sem=drecv.at[g * 2 + zh],
            device_id=fin(k),
            device_id_type=MESH,
        )

    def to_owner(g):
        for k in range(2):
            whole = hb[g, 4 * k + x0].astype(F32)
            for i in range(3):
                arrived(("x", g, i, k), xr.at[g, i, k])
                whole = whole + xr[g, i, k].astype(F32)
            rb[g, k] = whole.astype(BF)
        for k in range(2):

            @pl.when(fin_self(k))
            def _():
                fr[g, zh] = rb[g, k]

            @pl.when(jnp.logical_not(fin_self(k)))
            def _():
                d_copy(g, k).start()

    def finish_waits(g):
        for s in range(2):

            @pl.when(jnp.logical_not(jnp.logical_and(origin, zh == s)))
            def _():
                pltpu.make_async_remote_copy(
                    src_ref=fr.at[g, s],
                    dst_ref=fr.at[g, s],
                    send_sem=dsend.at[g * 2],
                    recv_sem=drecv.at[g * 2 + s],
                    device_id=cp,
                    device_id_type=MESH,
                ).wait_recv()

    def finish(g):
        finish_waits(g)
        gw_ref[:, g * CW : (g + 1) * CW] = fr[g, 0].astype(F32) + fr[g, 1].astype(F32)

    def f_copy(peer):
        return pltpu.make_async_remote_copy(
            src_ref=pvs.at[peer],
            dst_ref=pvr.at[d],
            send_sem=fsend.at[peer],
            recv_sem=frecv.at[d],
            device_id=at(peer, t),
            device_id_type=MESH,
        )

    def f_start(i, c):
        f_copy((d + i) % NDP).start()
        return c

    def f_wait(i, c):
        p = (d + i) % NDP
        pltpu.make_async_remote_copy(
            src_ref=pvr.at[p],
            dst_ref=pvr.at[p],
            send_sem=fsend.at[p],
            recv_sem=frecv.at[p],
            device_id=at(p, t),
            device_id_type=MESH,
        ).wait_recv()
        return c

    second(0)
    def turn(i, c):
        cols = pl.ds(pl.multiple_of(i * CW, CW), CW)
        xt[cols, :] = x[:, cols].T
        return c

    lax.fori_loop(0, 4, turn, 0)
    row = lax.broadcasted_iota(jnp.int32, (RB, 1), 0)
    slot = jnp.zeros((RB, 1), jnp.int32)
    length = jnp.ones((RB, 1), F32)
    advantage = jnp.zeros((RB, 1), F32)
    first = jnp.int32(0)
    for s in range(16):
        n = len_ref[0, 0, s]
        inside = jnp.logical_and(row >= first, row < first + n)
        slot = jnp.where(inside, row - first + bin_ref[0, 0, s] * SPAN, slot)
        length = jnp.where(inside, n.astype(F32), length)
        advantage = jnp.where(inside, adv_ref[0, 0, s], advantage)
        first = first + n
    importance = jnp.minimum(jnp.exp(to_col(gap_ref[...])), 2.0)
    coef_adv = (advantage * importance / length).astype(BF).astype(F32)
    coef_pull = (BETA / length).astype(BF).astype(F32)
    pick = (
        jnp.broadcast_to(slot, (RB, NDP * SPAN))
        == lax.broadcasted_iota(jnp.int32, (RB, NDP * SPAN), 1)
    ).astype(BF)
    slot_row = to_row(slot.astype(F32))
    place = (
        lax.broadcasted_iota(jnp.int32, (NDP * SPAN, RB), 0).astype(F32)
        == jnp.broadcast_to(slot_row, (NDP * SPAN, RB))
    ).astype(BF)

    w_share(0)
    policy(0)
    start(2)
    third(0)
    second(1)
    lax.fori_loop(1, NDP, e_start, 0)
    w_share(1)
    policy(1)
    start(3)
    second(2)
    finish_unit(0)
    third(1)
    third(2)

    def p_wait(i, c):
        p = (t + i) % 8
        pltpu.make_async_remote_copy(
            src_ref=pow_r.at[p],
            dst_ref=pow_r.at[p],
            send_sem=psend.at[p],
            recv_sem=precv.at[p],
            device_id=at(d, p),
            device_id_type=MESH,
        ).wait_recv()
        return c

    lax.fori_loop(1, 8, p_wait, 0)
    power = pow_r[0]
    for k in range(1, 8):
        power = power + pow_r[k]
    scale = to_col(lax.rsqrt(power[0:1, :] * (1.0 / WIDTH) + EPS))

    second(3)

    ld_cot.wait()

    def e_wait(i, c):
        p = (d + i) % NDP
        pltpu.make_async_remote_copy(
            src_ref=cr.at[p],
            dst_ref=cr.at[p],
            send_sem=esend.at[p],
            recv_sem=erecv.at[p],
            device_id=at(p, t),
            device_id_type=MESH,
        ).wait_recv()
        return c

    lax.fori_loop(1, NDP, e_wait, 0)

    finish_unit(2)
    slopes(0)
    finish_unit(1)
    spread(0)
    third(3)
    finish_unit(3)
    slopes(1)
    spread_far(0)
    spread(1)
    spread_end(0)
    reduce_core(0)
    spread_far(1)
    reduce_x(0)
    pvr[d] = pvs[d]
    lax.fori_loop(1, NDP, f_start, 0)
    spread_end(1)
    reduce_core(1)
    to_owner(0)
    reduce_x(1)
    to_owner(1)
    lax.fori_loop(1, NDP, f_wait, 0)
    pv_ref[0, 0] = pvr[...].reshape(NDP * SPAN, VW)
    finish(0)
    finish(1)

    for c in sent:
        c.wait_send()

    w_sent(0)
    w_sent(1)

    def p_done(i, c):
        p_copy((t + i) % 8).wait_send()
        return c

    def ef_done(i, c):
        e_copy((d + i) % NDP).wait_send()
        f_copy((d + i) % NDP).wait_send()
        return c

    lax.fori_loop(1, 8, p_done, 0)
    lax.fori_loop(1, NDP, ef_done, 0)
    for g in range(NG):
        for k in range(2):

            @pl.when(jnp.logical_not(fin_self(k)))
            def _():
                d_copy(g, k).wait_send()


def on_device(
    tokens,
    ref_gain,
    ref_weight,
    pol_gain,
    pol_weight,
    lengths,
    bins,
    advantage,
    logprob_gap,
    cotangent,
):
    any_spec = pl.BlockSpec(memory_space=pl.ANY)
    vmem = pl.BlockSpec(memory_space=pltpu.VMEM)
    smem = pl.BlockSpec(memory_space=pltpu.SMEM)
    dma = pltpu.SemaphoreType.DMA

    def buf(*shape, dtype=BF):
        return pltpu.VMEM(shape, dtype)

    return pl.pallas_call(
        kernel,
        out_shape=(
            jax.ShapeDtypeStruct(cotangent.shape, BF),
            jax.ShapeDtypeStruct((CHUNK, VW), F32),
        ),
        in_specs=[any_spec] * 4 + [vmem, vmem, smem, smem, smem, vmem],
        out_specs=(vmem, vmem),
        scratch_shapes=[
            buf(1024, FEAT),
            buf(FEAT, 1024),
            buf(FEAT, VW),
            buf(NG, FEAT, CW),
            buf(512, VW),
            buf(NG, FEAT, CW),
            buf(NG, FEAT, CW),
            buf(FEAT, 1, dtype=F32),
            buf(4, 2, 4, RB, CW),
            buf(4, 2, 2, HB, CW),
            buf(4, 2, 2, HB, CW),
            buf(4, 2, 2, HB, CW),
            buf(4, 3, 2, RB, CW),
            buf(4, 2, 2, HB, CW),
            buf(4, RB, CW),
            buf(4, RB, CW),
            buf(4, RB, CW, dtype=F32),
            buf(4, 4, RB, CW),
            buf(4, 4, RB, CW),
            buf(4, 2, HB, CW),
            buf(4, 2, HB, CW),
            buf(4, 2, HB, CW),
            buf(4, 2, HB, CW),
            buf(RB, VW, dtype=F32),
            buf(RB, VW, dtype=F32),
            buf(8, 8, RB, dtype=F32),
            buf(8, 8, RB, dtype=F32),
            buf(NDP, SPAN, VW),
            buf(NG, 2, 4, RB, CW),
            buf(NG, 2, 8, CHUNK, CW),
            buf(NG, 8, CHUNK, CW),
            buf(NG, 8, CHUNK, CW),
            buf(NG, 3, 2, CHUNK, CW),
            buf(NG, 2, CHUNK, CW),
            buf(NG, 2, CHUNK, CW),
            buf(NDP, SPAN, VW),
            buf(NDP, SPAN, VW),
            dma((4,)),
            dma((96,)),
            dma((96,)),
            dma((NG * 8,)),
            dma((NG * 8,)),
            dma((8,)),
            dma((8,)),
            dma((NDP,)),
            dma((NDP,)),
            dma((NDP,)),
            dma((NDP,)),
            dma((4,)),
            dma((4,)),
        ],
        compiler_params=pltpu.CompilerParams(collective_id=0, has_side_effects=True),
    )(
        tokens,
        ref_weight,
        pol_weight,
        cotangent,
        ref_gain.reshape(8, RB),
        pol_gain.reshape(8, 8, RB),
        lengths,
        bins,
        advantage,
        logprob_gap.reshape(1, RB),
    )


def solution(mesh):
    in_specs = (
        P("dp", "tensor"),
        P("tensor"),
        P("tensor", None),
        P(),
        P("dp", None),
        P("dp", "tensor", None),
        P("dp", "tensor", None),
        P("dp", "tensor", None),
        P(("dp", "tensor")),
        P("dp", "tensor", None, None),
    )
    out_specs = (P("dp", "tensor", None, None), P(("dp", "tensor"), None))
    return jax.shard_map(
        on_device, mesh=mesh, in_specs=in_specs, out_specs=out_specs, check_vma=False
    )
```

```python
import math

import jax
import jax.numpy as jnp
from jax import lax
from jax.experimental import pallas as pl
from jax.experimental.pallas import tpu as pltpu
from jax.sharding import PartitionSpec as P

EPS = 1e-06
BETA = 1.0
MESH = pl.DeviceIdType.MESH
BF = jnp.bfloat16
F32 = jnp.float32

FEAT = 1024
RB = 128
HB = RB // 2
VW = 512
CW = 256
NG = VW // CW
WIDTH = 8192
NDP = 16
SPAN = 16
AP = 64
MODES = "ezee"
CHUNK = 64


def kernel(
    x_hbm,
    rw_hbm,
    pw_hbm,
    cot_hbm,
    rg_ref,
    pg_ref,
    len_ref,
    bin_ref,
    adv_ref,
    gap_ref,
    pv_ref,
    gw_ref,
    x,
    xt,
    wr,
    wrs,
    pw,
    wp,
    wps,
    pgc,
    pb,
    ry1,
    ryd,
    ryc,
    re,
    ycb,
    qs,
    rz,
    tq,
    z1r,
    sb,
    zr1,
    zrd,
    zrc,
    zcb,
    tref,
    tpol,
    pow_s,
    pow_r,
    cr,
    ss,
    gb,
    dr0,
    hb,
    xr,
    rb,
    fr,
    pvs,
    pvr,
    loc,
    msend,
    mrecv,
    asend,
    arecv,
    psend,
    precv,
    esend,
    erecv,
    fsend,
    frecv,
    dsend,
    drecv,
):
    d = lax.axis_index("dp")
    t = lax.axis_index("tensor")
    core = d % 2
    xx = (d // 2) % 4
    zh = d // 8
    yy = t % 4
    zl = t // 4

    def at(dd, tt):
        return (dd, tt)

    yp = at(d, zl * 4 + (yy + 1) % 4)
    ym = at(d, zl * 4 + (yy + 3) % 4)
    yf = at(d, zl * 4 + (yy + 2) % 4)
    zp = at(d, (1 - zl) * 4 + yy)
    xp = at((zh * 4 + (xx + 1) % 4) * 2 + core, t)
    xm = at((zh * 4 + (xx + 3) % 4) * 2 + core, t)
    xf = at((zh * 4 + (xx + 2) % 4) * 2 + core, t)
    cp = at(d + 1 - 2 * core, t)
    same_z = zh == zl
    origin = jnp.logical_and(xx == yy, same_z)
    dfin = (zl * 4 + yy) * 2 + core

    def fin(k):
        return at(dfin, k * 4 + xx)

    def fin_src(s):
        return at((s * 4 + yy) * 2 + core, zh * 4 + xx)

    def fin_self(k):
        return jnp.logical_and(origin, zl == k)

    ld_rw = pltpu.make_async_copy(rw_hbm, wr, loc.at[0])
    ld_x = pltpu.make_async_copy(x_hbm, x, loc.at[1])
    ld_pw = pltpu.make_async_copy(pw_hbm, pw, loc.at[2])
    ld_cot = pltpu.make_async_copy(
        cot_hbm.at[0, 0, pl.ds(pl.multiple_of(d * SPAN, SPAN), SPAN), :], cr.at[d], loc.at[3]
    )
    ld_rw.start()
    ld_x.start()
    ld_pw.start()
    ld_cot.start()

    bar = pltpu.get_barrier_semaphore()

    def greet(dev):
        pl.semaphore_signal(bar, inc=1, device_id=dev, device_id_type=MESH)

    def greet_t(i, c):
        greet(at(d, (t + i) % 8))
        return c

    def greet_d(i, c):
        greet(at((d + i) % NDP, t))
        return c

    lax.fori_loop(1, 8, greet_t, 0)
    lax.fori_loop(1, NDP, greet_d, 0)

    def greet_w(i, c):
        @pl.when(jnp.logical_or(d // 2 != t, i != t))
        def _():
            greet(at(2 * t + core, i))

        return c

    lax.fori_loop(0, 8, greet_w, 0)

    for s in range(2):

        @pl.when(jnp.logical_not(jnp.logical_and(origin, zh == s)))
        def _():
            greet(fin_src(s))

    eye = lax.broadcasted_iota(jnp.int32, (RB, RB), 0) == lax.broadcasted_iota(
        jnp.int32, (RB, RB), 1
    )

    def to_col(row):
        return jnp.sum(
            jnp.where(eye, jnp.broadcast_to(row, (RB, RB)), 0.0), axis=1, keepdims=True
        )

    def to_row(col):
        return jnp.sum(
            jnp.where(eye, jnp.broadcast_to(col, (RB, RB)), 0.0), axis=0, keepdims=True
        )

    ld_rw.wait()
    for b in range(8):
        rows = slice(b * RB, (b + 1) * RB)
        gcol = to_col(rg_ref[b : b + 1, :])
        for g in range(NG):
            wrs[g, rows, :] = (wr[rows, g * CW : (g + 1) * CW].astype(F32) * gcol).astype(BF)
        pgc[rows, :] = to_col(pg_ref[t, b : b + 1, :])

    ld_x.wait()

    def products(u, weight):
        def step(i, c):
            rows = pl.ds(pl.multiple_of(i * CW, CW), CW)
            part = jnp.dot(x[rows, :], weight[...], preferred_element_type=F32).astype(BF)
            pb[u, i // 2, (i % 2) * 2] = part[:RB]
            pb[u, i // 2, (i % 2) * 2 + 1] = part[RB:]
            return c

        lax.fori_loop(0, 4, step, 0)

    sent = []
    ids = {}

    def copy(name, src, dst, dev):
        n = ids.setdefault(name, len(ids))
        c = pltpu.make_async_remote_copy(
            src_ref=src,
            dst_ref=dst,
            send_sem=msend.at[n],
            recv_sem=mrecv.at[n],
            device_id=dev,
            device_id_type=MESH,
        )
        c.start()
        sent.append(c)

    def arrived(name, landed):
        n = ids[name]
        pltpu.make_async_remote_copy(
            src_ref=landed,
            dst_ref=landed,
            send_sem=msend.at[n],
            recv_sem=mrecv.at[n],
            device_id=cp,
            device_id_type=MESH,
        ).wait_recv()

    y0, y1, y2, y3 = yy, (yy + 1) % 4, (yy + 2) % 4, (yy + 3) % 4

    def start_y(u):
        n = u
        copy(("y1", u, 0), pb.at[u, :, y2, 0:HB, :], ry1.at[n, 0], yp)
        copy(("y1", u, 1), pb.at[u, :, y2, HB:RB, :], ry1.at[n, 1], ym)
        copy(("yd", u, 0), pb.at[u, :, y1, HB:RB, :], ryd.at[n, 0], yp)
        copy(("yd", u, 1), pb.at[u, :, y3, 0:HB, :], ryd.at[n, 1], ym)

    def combine_y(u):
        n = u
        arrived(("y1", u, 0), ry1.at[n, 0])
        ycb[n, 0] = (pb[u, :, y1, 0:HB, :].astype(F32) + ry1[n, 0].astype(F32)).astype(BF)
        copy(("yc", u, 0), ycb.at[n, 0], ryc.at[n, 0], yp)
        arrived(("y1", u, 1), ry1.at[n, 1])
        ycb[n, 1] = (pb[u, :, y3, HB:RB, :].astype(F32) + ry1[n, 1].astype(F32)).astype(BF)
        copy(("yc", u, 1), ycb.at[n, 1], ryc.at[n, 1], ym)

    def cross_y(u):
        n = u
        for i in range(2):
            arrived(("yd", u, i), ryd.at[n, i])
        for i in range(2):
            arrived(("yc", u, i), ryc.at[n, i])

        def part(zt, lo):
            own = pb[u, zt, y0, lo : lo + HB, :].astype(F32)
            if lo == 0:
                return own + ryc[n, 0, zt].astype(F32) + ryd[n, 1, zt].astype(F32)
            return own + ryd[n, 0, zt].astype(F32) + ryc[n, 1, zt].astype(F32)

        qs[n, 0:HB, :] = part(1 - zl, 0).astype(BF)
        qs[n, HB:RB, :] = part(1 - zl, HB).astype(BF)
        copy(("yz", u), qs.at[n], rz.at[n], zp)
        tq[n, 0:HB, :] = part(zl, 0)
        tq[n, HB:RB, :] = part(zl, HB)

    def finish_y(u, total, g):
        n = u
        arrived(("yz", u), rz.at[n])
        total[:, g * CW : (g + 1) * CW] = tq[n] + rz[n].astype(F32)

    def start_z(u):
        n = u
        for o in (2, 1, 3, 0):
            copy(("z1", u, o), pb.at[u, 1 - zl, (yy + o) % 4], z1r.at[n, o], zp)

    def sum_z(u):
        n = u
        for o in (2, 1, 3):
            arrived(("z1", u, o), z1r.at[n, o])
            sb[n, o] = (pb[u, zl, (yy + o) % 4].astype(F32) + z1r[n, o].astype(F32)).astype(BF)
            if o == 2:
                copy(("zr", u, 0), sb.at[n, 2, 0:HB, :], zr1.at[n, 0], yp)
                copy(("zr", u, 1), sb.at[n, 2, HB:RB, :], zr1.at[n, 1], ym)
            elif o == 1:
                copy(("zd", u, 0), sb.at[n, 1, HB:RB, :], zrd.at[n, 0], yp)
            else:
                copy(("zd", u, 1), sb.at[n, 3, 0:HB, :], zrd.at[n, 1], ym)

    def combine_z(u):
        n = u
        arrived(("zr", u, 0), zr1.at[n, 0])
        zcb[n, 0] = (sb[n, 1, 0:HB, :].astype(F32) + zr1[n, 0].astype(F32)).astype(BF)
        copy(("zc", u, 0), zcb.at[n, 0], zrc.at[n, 0], yp)
        arrived(("zr", u, 1), zr1.at[n, 1])
        zcb[n, 1] = (sb[n, 3, HB:RB, :].astype(F32) + zr1[n, 1].astype(F32)).astype(BF)
        copy(("zc", u, 1), zcb.at[n, 1], zrc.at[n, 1], ym)

    def finish_z(u, total, g):
        n = u
        arrived(("z1", u, 0), z1r.at[n, 0])
        for i in range(2):
            arrived(("zd", u, i), zrd.at[n, i])
        for i in range(2):
            arrived(("zc", u, i), zrc.at[n, i])
        cols = slice(g * CW, (g + 1) * CW)
        own = pb[u, zl, y0].astype(F32) + z1r[n, 0].astype(F32)
        total[0:HB, cols] = own[0:HB] + zrc[n, 0].astype(F32) + zrd[n, 1].astype(F32)
        total[HB:RB, cols] = own[HB:RB] + zrd[n, 0].astype(F32) + zrc[n, 1].astype(F32)

    def start_e(u):
        copy(("e", u, 2), pb.at[u, :, y2], re.at[u, 2], yf)
        copy(("e", u, 0), pb.at[u, :, y1], re.at[u, 0], yp)
        copy(("e", u, 1), pb.at[u, :, y3], re.at[u, 1], ym)

    def none(u):
        pass

    def cross_e(u):
        for i in range(3):
            arrived(("e", u, i), re.at[u, i])

        def part(zt):
            whole = pb[u, zt, y0].astype(F32)
            for i in range(3):
                whole = whole + re[u, i, zt].astype(F32)
            return whole

        qs[u] = part(1 - zl).astype(BF)
        copy(("yz", u), qs.at[u], rz.at[u], zp)
        tq[u] = part(zl)

    def unit(u):
        if MODES[u] == "e":
            return start_e, none, cross_e, finish_y
        return (start_y, combine_y, cross_y, finish_y) if MODES[u] == "y" else (start_z, sum_z, combine_z, finish_z)

    def start(u):
        unit(u)[0](u)

    def second(u):
        unit(u)[1](u)

    def third(u):
        unit(u)[2](u)

    def finish_unit(u):
        unit(u)[3](u, (tref, tref, tpol, tpol)[u], u % 2)

    def w_copy(g, i):
        rank = (d // 2 + t + i) % 8
        return pltpu.make_async_remote_copy(
            src_ref=pw.at[
                pl.ds(pl.multiple_of(t * AP, AP), AP), g * CW : (g + 1) * CW
            ],
            dst_ref=wp.at[g, pl.ds(pl.multiple_of(core * 512 + t * AP, AP), AP), :],
            send_sem=asend.at[g * 8 + rank],
            recv_sem=arecv.at[g * 8 + t],
            device_id=at(rank * 2 + core, d // 2),
            device_id_type=MESH,
        )

    def w_remote(i):
        return jnp.logical_or(d // 2 != t, (d // 2 + t + i) % 8 != d // 2)

    def w_start(g):
        def step(i, c):
            @pl.when(w_remote(i))
            def _():
                w_copy(g, i).start()

            return c

        lax.fori_loop(0, 8, step, 0)

    def w_sent(g):
        def step(i, c):
            @pl.when(w_remote(i))
            def _():
                w_copy(g, i).wait_send()

            return c

        lax.fori_loop(0, 8, step, 0)

    def w_share(g):
        def step(i, c):
            part = wp.at[g, pl.ds(pl.multiple_of(core * 512 + i * AP, AP), AP), :]

            @pl.when(jnp.logical_or(d // 2 != t, i != t))
            def _():
                pltpu.make_async_remote_copy(
                    src_ref=part,
                    dst_ref=part,
                    send_sem=asend.at[g * 8 + i],
                    recv_sem=arecv.at[g * 8 + i],
                    device_id=cp,
                    device_id_type=MESH,
                ).wait_recv()

            return c

        lax.fori_loop(0, 8, step, 0)
        mine = wp.at[g, pl.ds(pl.multiple_of(core * 512, 512), 512), :]
        copy(("w", g), mine, mine, cp)

    products(0, wrs.at[0])
    products(1, wrs.at[1])

    ld_pw.wait()

    @pl.when(d // 2 == t)
    def _():
        for g in range(NG):
            wp[g, pl.ds(pl.multiple_of(core * 512 + t * AP, AP), AP), :] = pw[
                pl.ds(pl.multiple_of(t * AP, AP), AP), g * CW : (g + 1) * CW
            ]

    pl.semaphore_wait(
        bar,
        30
        - jnp.where(d // 2 == t, 1, 0)
        + jnp.where(fin_self(0), 0, 1)
        + jnp.where(fin_self(1), 0, 1),
    )


    w_start(0)
    start(0)
    w_start(1)
    start(1)

    def squares(b, c):
        rows = pl.ds(pl.multiple_of(b * RB, RB), RB)
        xb = x[rows, :].astype(F32)
        part = jnp.sum(xb * xb, axis=1, keepdims=True)
        pow_s[b] = jnp.broadcast_to(to_row(part), (8, RB))
        return c

    lax.fori_loop(0, 8, squares, 0)
    pow_r[t] = pow_s[t]

    def p_copy(peer):
        return pltpu.make_async_remote_copy(
            src_ref=pow_s.at[peer],
            dst_ref=pow_r.at[t],
            send_sem=psend.at[peer],
            recv_sem=precv.at[t],
            device_id=at(d, peer),
            device_id_type=MESH,
        )

    def p_start(i, c):
        p_copy((t + i) % 8).start()
        return c

    lax.fori_loop(1, 8, p_start, 0)


    def e_copy(peer):
        return pltpu.make_async_remote_copy(
            src_ref=cot_hbm.at[0, 0, pl.ds(pl.multiple_of(peer * SPAN, SPAN), SPAN), :],
            dst_ref=cr.at[d],
            send_sem=esend.at[peer],
            recv_sem=erecv.at[d],
            device_id=at(peer, t),
            device_id_type=MESH,
        )

    def e_start(i, c):
        e_copy((d + i) % NDP).start()
        return c

    def policy(g):
        arrived(("w", g), wp.at[g, pl.ds(pl.multiple_of((1 - core) * 512, 512), 512), :])
        for b in range(8):
            rows = slice(b * RB, (b + 1) * RB)
            wps[g, rows, :] = (wp[g, rows, :].astype(F32) * pgc[rows, :]).astype(BF)
        products(2 + g, wps.at[g])

    def slopes(g):
        cols = slice(g * CW, (g + 1) * CW)
        upstream = jnp.dot(
            pick, cr[:, :, cols].reshape(NDP * SPAN, CW), preferred_element_type=F32
        )
        values = tpol[:, cols] * scale
        ref_values = (tref[:, cols] * scale).astype(BF).astype(F32)
        slope = coef_adv * upstream + coef_pull * (values - ref_values)
        ss[g, zl, y0] = (slope * scale).astype(BF)
        mine = ss.at[g, zl, y0]
        copy(("cf", g), mine, mine, yf)
        copy(("cz", g), mine, mine, zp)
        copy(("cp", g), mine, mine, yp)
        copy(("cm", g), mine, mine, ym)
        out = jnp.dot(place, values.astype(BF), preferred_element_type=F32).astype(BF)
        pvs[:, :, cols] = out.reshape(NDP, SPAN, CW)

    def spread(g):
        oz = 1 - zl
        arrived(("cz", g), ss.at[g, oz, y0])
        block = ss.at[g, oz, y0]
        copy(("czp", g), block, block, yp)
        copy(("czm", g), block, block, ym)

    def spread_far(g):
        block = ss.at[g, zl, y2]
        arrived(("cf", g), block)
        copy(("czz", g), block, block, zp)

    def spread_end(g):
        oz = 1 - zl
        arrived(("cp", g), ss.at[g, zl, y3])
        arrived(("cm", g), ss.at[g, zl, y1])
        arrived(("czp", g), ss.at[g, oz, y3])
        arrived(("czm", g), ss.at[g, oz, y1])
        arrived(("czz", g), ss.at[g, oz, y2])

    factor = 1.0 / math.sqrt(2048.0)

    def gradient(g, half):
        def step(i, c):
            base = pl.multiple_of((half * 2 + i) * CW, CW)
            rows = pl.ds(base, CW)
            part = jnp.dot(
                xt[rows, :], ss[g].reshape(FEAT, CW), preferred_element_type=F32
            )
            part = (part * (pgc[rows, :] * factor)).astype(BF)
            gb[g, half, pl.ds(pl.multiple_of(i * 4, 4), 4)] = part.reshape(4, CHUNK, CW)
            return c

        lax.fori_loop(0, 2, step, 0)

    def reduce_core(g):
        gradient(g, 1 - core)
        copy(("d0", g), gb.at[g, 1 - core], dr0.at[g], cp)
        gradient(g, core)

    x0, x1, x2, x3 = xx, (xx + 1) % 4, (xx + 2) % 4, (xx + 3) % 4

    def reduce_x(g):
        arrived(("d0", g), dr0.at[g])
        hb[g] = (gb[g, core].astype(F32) + dr0[g].astype(F32)).astype(BF)
        for i, (quarter, dev) in enumerate(((x2, xf), (x1, xp), (x3, xm))):
            for k in range(2):
                copy(("x", g, i, k), hb.at[g, 4 * k + quarter], xr.at[g, i, k], dev)

    def d_copy(g, k):
        return pltpu.make_async_remote_copy(
            src_ref=rb.at[g, k],
            dst_ref=fr.at[g, zh],
            send_sem=dsend.at[g * 2 + k],
            recv_sem=drecv.at[g * 2 + zh],
            device_id=fin(k),
            device_id_type=MESH,
        )

    def to_owner(g):
        for k in range(2):
            whole = hb[g, 4 * k + x0].astype(F32)
            for i in range(3):
                arrived(("x", g, i, k), xr.at[g, i, k])
                whole = whole + xr[g, i, k].astype(F32)
            rb[g, k] = whole.astype(BF)
        for k in range(2):

            @pl.when(fin_self(k))
            def _():
                fr[g, zh] = rb[g, k]

            @pl.when(jnp.logical_not(fin_self(k)))
            def _():
                d_copy(g, k).start()

    def finish_waits(g):
        for s in range(2):

            @pl.when(jnp.logical_not(jnp.logical_and(origin, zh == s)))
            def _():
                pltpu.make_async_remote_copy(
                    src_ref=fr.at[g, s],
                    dst_ref=fr.at[g, s],
                    send_sem=dsend.at[g * 2],
                    recv_sem=drecv.at[g * 2 + s],
                    device_id=cp,
                    device_id_type=MESH,
                ).wait_recv()

    def finish(g):
        finish_waits(g)
        gw_ref[:, g * CW : (g + 1) * CW] = fr[g, 0].astype(F32) + fr[g, 1].astype(F32)

    def f_copy(peer):
        return pltpu.make_async_remote_copy(
            src_ref=pvs.at[peer],
            dst_ref=pvr.at[d],
            send_sem=fsend.at[peer],
            recv_sem=frecv.at[d],
            device_id=at(peer, t),
            device_id_type=MESH,
        )

    def f_start(i, c):
        f_copy((d + i) % NDP).start()
        return c

    def f_wait(i, c):
        p = (d + i) % NDP
        pltpu.make_async_remote_copy(
            src_ref=pvr.at[p],
            dst_ref=pvr.at[p],
            send_sem=fsend.at[p],
            recv_sem=frecv.at[p],
            device_id=at(p, t),
            device_id_type=MESH,
        ).wait_recv()
        return c

    lax.fori_loop(1, NDP, e_start, 0)
    second(0)
    def turn(i, c):
        cols = pl.ds(pl.multiple_of(i * CW, CW), CW)
        xt[cols, :] = x[:, cols].T
        return c

    lax.fori_loop(0, 4, turn, 0)
    row = lax.broadcasted_iota(jnp.int32, (RB, 1), 0)
    slot = jnp.zeros((RB, 1), jnp.int32)
    length = jnp.ones((RB, 1), F32)
    advantage = jnp.zeros((RB, 1), F32)
    first = jnp.int32(0)
    for s in range(16):
        n = len_ref[0, 0, s]
        inside = jnp.logical_and(row >= first, row < first + n)
        slot = jnp.where(inside, row - first + bin_ref[0, 0, s] * SPAN, slot)
        length = jnp.where(inside, n.astype(F32), length)
        advantage = jnp.where(inside, adv_ref[0, 0, s], advantage)
        first = first + n
    importance = jnp.minimum(jnp.exp(to_col(gap_ref[...])), 2.0)
    coef_adv = (advantage * importance / length).astype(BF).astype(F32)
    coef_pull = (BETA / length).astype(BF).astype(F32)
    pick = (
        jnp.broadcast_to(slot, (RB, NDP * SPAN))
        == lax.broadcasted_iota(jnp.int32, (RB, NDP * SPAN), 1)
    ).astype(BF)
    slot_row = to_row(slot.astype(F32))
    place = (
        lax.broadcasted_iota(jnp.int32, (NDP * SPAN, RB), 0).astype(F32)
        == jnp.broadcast_to(slot_row, (NDP * SPAN, RB))
    ).astype(BF)

    w_share(0)
    policy(0)
    start(2)
    third(0)
    second(1)
    w_share(1)
    policy(1)
    start(3)
    second(2)
    finish_unit(0)
    third(1)
    third(2)

    def p_wait(i, c):
        p = (t + i) % 8
        pltpu.make_async_remote_copy(
            src_ref=pow_r.at[p],
            dst_ref=pow_r.at[p],
            send_sem=psend.at[p],
            recv_sem=precv.at[p],
            device_id=at(d, p),
            device_id_type=MESH,
        ).wait_recv()
        return c

    lax.fori_loop(1, 8, p_wait, 0)
    power = pow_r[0]
    for k in range(1, 8):
        power = power + pow_r[k]
    scale = to_col(lax.rsqrt(power[0:1, :] * (1.0 / WIDTH) + EPS))

    second(3)

    ld_cot.wait()

    def e_wait(i, c):
        p = (d + i) % NDP
        pltpu.make_async_remote_copy(
            src_ref=cr.at[p],
            dst_ref=cr.at[p],
            send_sem=esend.at[p],
            recv_sem=erecv.at[p],
            device_id=at(p, t),
            device_id_type=MESH,
        ).wait_recv()
        return c

    lax.fori_loop(1, NDP, e_wait, 0)

    finish_unit(2)
    slopes(0)
    finish_unit(1)
    spread(0)
    third(3)
    finish_unit(3)
    slopes(1)
    spread_far(0)
    spread(1)
    spread_end(0)
    reduce_core(0)
    spread_far(1)
    reduce_x(0)
    pvr[d] = pvs[d]
    lax.fori_loop(1, NDP, f_start, 0)
    spread_end(1)
    reduce_core(1)
    to_owner(0)
    reduce_x(1)
    to_owner(1)
    lax.fori_loop(1, NDP, f_wait, 0)
    pv_ref[0, 0] = pvr[...].reshape(NDP * SPAN, VW)
    finish(0)
    finish(1)

    for c in sent:
        c.wait_send()

    w_sent(0)
    w_sent(1)

    def p_done(i, c):
        p_copy((t + i) % 8).wait_send()
        return c

    def ef_done(i, c):
        e_copy((d + i) % NDP).wait_send()
        f_copy((d + i) % NDP).wait_send()
        return c

    lax.fori_loop(1, 8, p_done, 0)
    lax.fori_loop(1, NDP, ef_done, 0)
    for g in range(NG):
        for k in range(2):

            @pl.when(jnp.logical_not(fin_self(k)))
            def _():
                d_copy(g, k).wait_send()


def hand_over(packed_ref, grads_ref, pv_ref, gw_ref):
    pv_ref[...] = packed_ref[...]
    gw_ref[...] = grads_ref[...]


def on_device(
    tokens,
    ref_gain,
    ref_weight,
    pol_gain,
    pol_weight,
    lengths,
    bins,
    advantage,
    logprob_gap,
    cotangent,
):
    any_spec = pl.BlockSpec(memory_space=pl.ANY)
    vmem = pl.BlockSpec(memory_space=pltpu.VMEM)
    smem = pl.BlockSpec(memory_space=pltpu.SMEM)
    dma = pltpu.SemaphoreType.DMA

    def buf(*shape, dtype=BF):
        return pltpu.VMEM(shape, dtype)

    packed, grads = pl.pallas_call(
        kernel,
        out_shape=(
            jax.ShapeDtypeStruct(cotangent.shape, BF),
            jax.ShapeDtypeStruct((CHUNK, VW), F32),
        ),
        in_specs=[any_spec] * 4 + [vmem, vmem, smem, smem, smem, vmem],
        out_specs=(vmem, vmem),
        scratch_shapes=[
            buf(1024, FEAT),
            buf(FEAT, 1024),
            buf(FEAT, VW),
            buf(NG, FEAT, CW),
            buf(512, VW),
            buf(NG, FEAT, CW),
            buf(NG, FEAT, CW),
            buf(FEAT, 1, dtype=F32),
            buf(4, 2, 4, RB, CW),
            buf(4, 2, 2, HB, CW),
            buf(4, 2, 2, HB, CW),
            buf(4, 2, 2, HB, CW),
            buf(4, 3, 2, RB, CW),
            buf(4, 2, 2, HB, CW),
            buf(4, RB, CW),
            buf(4, RB, CW),
            buf(4, RB, CW, dtype=F32),
            buf(4, 4, RB, CW),
            buf(4, 4, RB, CW),
            buf(4, 2, HB, CW),
            buf(4, 2, HB, CW),
            buf(4, 2, HB, CW),
            buf(4, 2, HB, CW),
            buf(RB, VW, dtype=F32),
            buf(RB, VW, dtype=F32),
            buf(8, 8, RB, dtype=F32),
            buf(8, 8, RB, dtype=F32),
            buf(NDP, SPAN, VW),
            buf(NG, 2, 4, RB, CW),
            buf(NG, 2, 8, CHUNK, CW),
            buf(NG, 8, CHUNK, CW),
            buf(NG, 8, CHUNK, CW),
            buf(NG, 3, 2, CHUNK, CW),
            buf(NG, 2, CHUNK, CW),
            buf(NG, 2, CHUNK, CW),
            buf(NDP, SPAN, VW),
            buf(NDP, SPAN, VW),
            dma((4,)),
            dma((96,)),
            dma((96,)),
            dma((NG * 8,)),
            dma((NG * 8,)),
            dma((8,)),
            dma((8,)),
            dma((NDP,)),
            dma((NDP,)),
            dma((NDP,)),
            dma((NDP,)),
            dma((4,)),
            dma((4,)),
        ],
        compiler_params=pltpu.CompilerParams(collective_id=0, has_side_effects=True),
    )(
        tokens,
        ref_weight,
        pol_weight,
        cotangent,
        ref_gain.reshape(8, RB),
        pol_gain.reshape(8, 8, RB),
        lengths,
        bins,
        advantage,
        logprob_gap.reshape(1, RB),
    )
    return pl.pallas_call(
        hand_over,
        out_shape=(
            jax.ShapeDtypeStruct(cotangent.shape, BF),
            jax.ShapeDtypeStruct((CHUNK, VW), F32),
        ),
        in_specs=[vmem, vmem],
        out_specs=(vmem, vmem),
    )(packed, grads)


def solution(mesh):
    in_specs = (
        P("dp", "tensor"),
        P("tensor"),
        P("tensor", None),
        P(),
        P("dp", None),
        P("dp", "tensor", None),
        P("dp", "tensor", None),
        P("dp", "tensor", None),
        P(("dp", "tensor")),
        P("dp", "tensor", None, None),
    )
    out_specs = (P("dp", "tensor", None, None), P(("dp", "tensor"), None))
    return jax.shard_map(
        on_device, mesh=mesh, in_specs=in_specs, out_specs=out_specs, check_vma=False
    )
```

```python
import math

import jax
import jax.numpy as jnp
from jax import lax
from jax.experimental import pallas as pl
from jax.experimental.pallas import tpu as pltpu
from jax.sharding import PartitionSpec as P

EPS = 1e-06
BETA = 1.0
MESH = pl.DeviceIdType.MESH
BF = jnp.bfloat16
F32 = jnp.float32

FEAT = 1024
RB = 128
HB = RB // 2
VW = 512
CW = 256
NG = VW // CW
WIDTH = 8192
NDP = 16
SPAN = 16
AP = 64
MODES = "ezee"
CHUNK = 64


def kernel(
    x_hbm,
    rw_hbm,
    pw_hbm,
    cot_hbm,
    rg_ref,
    pg_ref,
    len_ref,
    bin_ref,
    adv_ref,
    gap_ref,
    pv_ref,
    gw_ref,
    x,
    xt,
    wr,
    wrs,
    pw,
    wp,
    wps,
    pgc,
    pb,
    ry1,
    ryd,
    ryc,
    re,
    ycb,
    qs,
    rz,
    tq,
    z1r,
    sb,
    zr1,
    zrd,
    zrc,
    zcb,
    tref,
    tpol,
    pow_s,
    pow_r,
    cr,
    ss,
    gb,
    dr0,
    hb,
    xr,
    rb,
    fr,
    pvs,
    pvr,
    loc,
    msend,
    mrecv,
    asend,
    arecv,
    psend,
    precv,
    esend,
    erecv,
    fsend,
    frecv,
    dsend,
    drecv,
):
    d = lax.axis_index("dp")
    t = lax.axis_index("tensor")
    core = d % 2
    xx = (d // 2) % 4
    zh = d // 8
    yy = t % 4
    zl = t // 4

    def at(dd, tt):
        return (dd, tt)

    yp = at(d, zl * 4 + (yy + 1) % 4)
    ym = at(d, zl * 4 + (yy + 3) % 4)
    yf = at(d, zl * 4 + (yy + 2) % 4)
    zp = at(d, (1 - zl) * 4 + yy)
    xp = at((zh * 4 + (xx + 1) % 4) * 2 + core, t)
    xm = at((zh * 4 + (xx + 3) % 4) * 2 + core, t)
    xf = at((zh * 4 + (xx + 2) % 4) * 2 + core, t)
    cp = at(d + 1 - 2 * core, t)
    same_z = zh == zl
    origin = jnp.logical_and(xx == yy, same_z)
    dfin = (zl * 4 + yy) * 2 + core

    def fin(k):
        return at(dfin, k * 4 + xx)

    def fin_src(s):
        return at((s * 4 + yy) * 2 + core, zh * 4 + xx)

    def fin_self(k):
        return jnp.logical_and(origin, zl == k)

    ld_rw = pltpu.make_async_copy(rw_hbm, wr, loc.at[0])
    ld_x = pltpu.make_async_copy(x_hbm, x, loc.at[1])
    ld_pw = pltpu.make_async_copy(pw_hbm, pw, loc.at[2])
    ld_cot = pltpu.make_async_copy(
        cot_hbm.at[0, 0, pl.ds(pl.multiple_of(d * SPAN, SPAN), SPAN), :], cr.at[d], loc.at[3]
    )

    bar = pltpu.get_barrier_semaphore()

    def greet(dev):
        pl.semaphore_signal(bar, inc=1, device_id=dev, device_id_type=MESH)

    def greet_t(i, c):
        greet(at(d, (t + i) % 8))
        return c

    def greet_d(i, c):
        greet(at((d + i) % NDP, t))
        return c


    def greet_w(i, c):
        @pl.when(jnp.logical_or(d // 2 != t, i != t))
        def _():
            greet(at(2 * t + core, i))

        return c

    lax.fori_loop(0, 8, greet_w, 0, unroll=True)

    for s in range(2):

        @pl.when(jnp.logical_not(jnp.logical_and(origin, zh == s)))
        def _():
            greet(fin_src(s))

    lax.fori_loop(1, 8, greet_t, 0, unroll=True)
    lax.fori_loop(1, NDP, greet_d, 0, unroll=True)
    ld_rw.start()
    ld_x.start()
    ld_pw.start()
    ld_cot.start()

    eye = lax.broadcasted_iota(jnp.int32, (RB, RB), 0) == lax.broadcasted_iota(
        jnp.int32, (RB, RB), 1
    )

    def to_col(row):
        return jnp.sum(
            jnp.where(eye, jnp.broadcast_to(row, (RB, RB)), 0.0), axis=1, keepdims=True
        )

    def to_row(col):
        return jnp.sum(
            jnp.where(eye, jnp.broadcast_to(col, (RB, RB)), 0.0), axis=0, keepdims=True
        )

    ld_rw.wait()
    for b in range(8):
        rows = slice(b * RB, (b + 1) * RB)
        gcol = to_col(rg_ref[b : b + 1, :])
        for g in range(NG):
            wrs[g, rows, :] = (wr[rows, g * CW : (g + 1) * CW].astype(F32) * gcol).astype(BF)
        pgc[rows, :] = to_col(pg_ref[t, b : b + 1, :])

    ld_x.wait()

    def products(u, weight):
        def step(i, c):
            rows = pl.ds(pl.multiple_of(i * CW, CW), CW)
            part = jnp.dot(x[rows, :], weight[...], preferred_element_type=F32).astype(BF)
            pb[u, i // 2, (i % 2) * 2] = part[:RB]
            pb[u, i // 2, (i % 2) * 2 + 1] = part[RB:]
            return c

        lax.fori_loop(0, 4, step, 0)

    sent = []
    ids = {}

    def copy(name, src, dst, dev):
        n = ids.setdefault(name, len(ids))
        c = pltpu.make_async_remote_copy(
            src_ref=src,
            dst_ref=dst,
            send_sem=msend.at[n],
            recv_sem=mrecv.at[n],
            device_id=dev,
            device_id_type=MESH,
        )
        c.start()
        sent.append(c)

    def arrived(name, landed):
        n = ids[name]
        pltpu.make_async_remote_copy(
            src_ref=landed,
            dst_ref=landed,
            send_sem=msend.at[n],
            recv_sem=mrecv.at[n],
            device_id=cp,
            device_id_type=MESH,
        ).wait_recv()

    y0, y1, y2, y3 = yy, (yy + 1) % 4, (yy + 2) % 4, (yy + 3) % 4

    def start_y(u):
        n = u
        copy(("y1", u, 0), pb.at[u, :, y2, 0:HB, :], ry1.at[n, 0], yp)
        copy(("y1", u, 1), pb.at[u, :, y2, HB:RB, :], ry1.at[n, 1], ym)
        copy(("yd", u, 0), pb.at[u, :, y1, HB:RB, :], ryd.at[n, 0], yp)
        copy(("yd", u, 1), pb.at[u, :, y3, 0:HB, :], ryd.at[n, 1], ym)

    def combine_y(u):
        n = u
        arrived(("y1", u, 0), ry1.at[n, 0])
        ycb[n, 0] = (pb[u, :, y1, 0:HB, :].astype(F32) + ry1[n, 0].astype(F32)).astype(BF)
        copy(("yc", u, 0), ycb.at[n, 0], ryc.at[n, 0], yp)
        arrived(("y1", u, 1), ry1.at[n, 1])
        ycb[n, 1] = (pb[u, :, y3, HB:RB, :].astype(F32) + ry1[n, 1].astype(F32)).astype(BF)
        copy(("yc", u, 1), ycb.at[n, 1], ryc.at[n, 1], ym)

    def cross_y(u):
        n = u
        for i in range(2):
            arrived(("yd", u, i), ryd.at[n, i])
        for i in range(2):
            arrived(("yc", u, i), ryc.at[n, i])

        def part(zt, lo):
            own = pb[u, zt, y0, lo : lo + HB, :].astype(F32)
            if lo == 0:
                return own + ryc[n, 0, zt].astype(F32) + ryd[n, 1, zt].astype(F32)
            return own + ryd[n, 0, zt].astype(F32) + ryc[n, 1, zt].astype(F32)

        qs[n, 0:HB, :] = part(1 - zl, 0).astype(BF)
        qs[n, HB:RB, :] = part(1 - zl, HB).astype(BF)
        copy(("yz", u), qs.at[n], rz.at[n], zp)
        tq[n, 0:HB, :] = part(zl, 0)
        tq[n, HB:RB, :] = part(zl, HB)

    def finish_y(u, total, g):
        n = u
        arrived(("yz", u), rz.at[n])
        total[:, g * CW : (g + 1) * CW] = tq[n] + rz[n].astype(F32)

    def start_z(u):
        n = u
        for o in (2, 1, 3, 0):
            copy(("z1", u, o), pb.at[u, 1 - zl, (yy + o) % 4], z1r.at[n, o], zp)

    def sum_z(u):
        n = u
        for o in (2, 1, 3):
            arrived(("z1", u, o), z1r.at[n, o])
            sb[n, o] = (pb[u, zl, (yy + o) % 4].astype(F32) + z1r[n, o].astype(F32)).astype(BF)
            if o == 2:
                copy(("zr", u, 0), sb.at[n, 2, 0:HB, :], zr1.at[n, 0], yp)
                copy(("zr", u, 1), sb.at[n, 2, HB:RB, :], zr1.at[n, 1], ym)
            elif o == 1:
                copy(("zd", u, 0), sb.at[n, 1, HB:RB, :], zrd.at[n, 0], yp)
            else:
                copy(("zd", u, 1), sb.at[n, 3, 0:HB, :], zrd.at[n, 1], ym)

    def combine_z(u):
        n = u
        arrived(("zr", u, 0), zr1.at[n, 0])
        zcb[n, 0] = (sb[n, 1, 0:HB, :].astype(F32) + zr1[n, 0].astype(F32)).astype(BF)
        copy(("zc", u, 0), zcb.at[n, 0], zrc.at[n, 0], yp)
        arrived(("zr", u, 1), zr1.at[n, 1])
        zcb[n, 1] = (sb[n, 3, HB:RB, :].astype(F32) + zr1[n, 1].astype(F32)).astype(BF)
        copy(("zc", u, 1), zcb.at[n, 1], zrc.at[n, 1], ym)

    def finish_z(u, total, g):
        n = u
        arrived(("z1", u, 0), z1r.at[n, 0])
        for i in range(2):
            arrived(("zd", u, i), zrd.at[n, i])
        for i in range(2):
            arrived(("zc", u, i), zrc.at[n, i])
        cols = slice(g * CW, (g + 1) * CW)
        own = pb[u, zl, y0].astype(F32) + z1r[n, 0].astype(F32)
        total[0:HB, cols] = own[0:HB] + zrc[n, 0].astype(F32) + zrd[n, 1].astype(F32)
        total[HB:RB, cols] = own[HB:RB] + zrd[n, 0].astype(F32) + zrc[n, 1].astype(F32)

    def start_e(u):
        copy(("e", u, 2), pb.at[u, :, y2], re.at[u, 2], yf)
        copy(("e", u, 0), pb.at[u, :, y1], re.at[u, 0], yp)
        copy(("e", u, 1), pb.at[u, :, y3], re.at[u, 1], ym)

    def none(u):
        pass

    def cross_e(u):
        for i in range(3):
            arrived(("e", u, i), re.at[u, i])

        def part(zt):
            whole = pb[u, zt, y0].astype(F32)
            for i in range(3):
                whole = whole + re[u, i, zt].astype(F32)
            return whole

        qs[u] = part(1 - zl).astype(BF)
        copy(("yz", u), qs.at[u], rz.at[u], zp)
        tq[u] = part(zl)

    def unit(u):
        if MODES[u] == "e":
            return start_e, none, cross_e, finish_y
        return (start_y, combine_y, cross_y, finish_y) if MODES[u] == "y" else (start_z, sum_z, combine_z, finish_z)

    def start(u):
        unit(u)[0](u)

    def second(u):
        unit(u)[1](u)

    def third(u):
        unit(u)[2](u)

    def finish_unit(u):
        unit(u)[3](u, (tref, tref, tpol, tpol)[u], u % 2)

    def w_copy(g, i):
        rank = (d // 2 + t + i) % 8
        return pltpu.make_async_remote_copy(
            src_ref=pw.at[
                pl.ds(pl.multiple_of(t * AP, AP), AP), g * CW : (g + 1) * CW
            ],
            dst_ref=wp.at[g, pl.ds(pl.multiple_of(core * 512 + t * AP, AP), AP), :],
            send_sem=asend.at[g * 8 + rank],
            recv_sem=arecv.at[g * 8 + t],
            device_id=at(rank * 2 + core, d // 2),
            device_id_type=MESH,
        )

    def w_remote(i):
        return jnp.logical_or(d // 2 != t, (d // 2 + t + i) % 8 != d // 2)

    def w_start(g):
        def step(i, c):
            @pl.when(w_remote(i))
            def _():
                w_copy(g, i).start()

            return c

        lax.fori_loop(0, 8, step, 0)

    def w_sent(g):
        def step(i, c):
            @pl.when(w_remote(i))
            def _():
                w_copy(g, i).wait_send()

            return c

        lax.fori_loop(0, 8, step, 0)

    def w_share(g):
        def step(i, c):
            part = wp.at[g, pl.ds(pl.multiple_of(core * 512 + i * AP, AP), AP), :]

            @pl.when(jnp.logical_or(d // 2 != t, i != t))
            def _():
                pltpu.make_async_remote_copy(
                    src_ref=part,
                    dst_ref=part,
                    send_sem=asend.at[g * 8 + i],
                    recv_sem=arecv.at[g * 8 + i],
                    device_id=cp,
                    device_id_type=MESH,
                ).wait_recv()

            return c

        lax.fori_loop(0, 8, step, 0)
        mine = wp.at[g, pl.ds(pl.multiple_of(core * 512, 512), 512), :]
        copy(("w", g), mine, mine, cp)

    products(0, wrs.at[0])
    products(1, wrs.at[1])

    ld_pw.wait()

    @pl.when(d // 2 == t)
    def _():
        for g in range(NG):
            wp[g, pl.ds(pl.multiple_of(core * 512 + t * AP, AP), AP), :] = pw[
                pl.ds(pl.multiple_of(t * AP, AP), AP), g * CW : (g + 1) * CW
            ]

    pl.semaphore_wait(
        bar,
        30
        - jnp.where(d // 2 == t, 1, 0)
        + jnp.where(fin_self(0), 0, 1)
        + jnp.where(fin_self(1), 0, 1),
    )


    w_start(0)
    start(0)
    w_start(1)
    start(1)

    def squares(b, c):
        rows = pl.ds(pl.multiple_of(b * RB, RB), RB)
        xb = x[rows, :].astype(F32)
        part = jnp.sum(xb * xb, axis=1, keepdims=True)
        pow_s[b] = jnp.broadcast_to(to_row(part), (8, RB))
        return c

    lax.fori_loop(0, 8, squares, 0)
    pow_r[t] = pow_s[t]

    def p_copy(peer):
        return pltpu.make_async_remote_copy(
            src_ref=pow_s.at[peer],
            dst_ref=pow_r.at[t],
            send_sem=psend.at[peer],
            recv_sem=precv.at[t],
            device_id=at(d, peer),
            device_id_type=MESH,
        )

    def p_start(i, c):
        p_copy((t + i) % 8).start()
        return c

    lax.fori_loop(1, 8, p_start, 0)


    def e_copy(peer):
        return pltpu.make_async_remote_copy(
            src_ref=cot_hbm.at[0, 0, pl.ds(pl.multiple_of(peer * SPAN, SPAN), SPAN), :],
            dst_ref=cr.at[d],
            send_sem=esend.at[peer],
            recv_sem=erecv.at[d],
            device_id=at(peer, t),
            device_id_type=MESH,
        )

    def e_start(i, c):
        e_copy((d + i) % NDP).start()
        return c

    def policy(g):
        arrived(("w", g), wp.at[g, pl.ds(pl.multiple_of((1 - core) * 512, 512), 512), :])
        for b in range(8):
            rows = slice(b * RB, (b + 1) * RB)
            wps[g, rows, :] = (wp[g, rows, :].astype(F32) * pgc[rows, :]).astype(BF)
        products(2 + g, wps.at[g])

    def slopes(g):
        cols = slice(g * CW, (g + 1) * CW)
        upstream = jnp.dot(
            pick, cr[:, :, cols].reshape(NDP * SPAN, CW), preferred_element_type=F32
        )
        values = tpol[:, cols] * scale
        ref_values = (tref[:, cols] * scale).astype(BF).astype(F32)
        slope = coef_adv * upstream + coef_pull * (values - ref_values)
        ss[g, zl, y0] = (slope * scale).astype(BF)
        mine = ss.at[g, zl, y0]
        copy(("cf", g), mine, mine, yf)
        copy(("cz", g), mine, mine, zp)
        copy(("cp", g), mine, mine, yp)
        copy(("cm", g), mine, mine, ym)
        out = jnp.dot(place, values.astype(BF), preferred_element_type=F32).astype(BF)
        pvs[:, :, cols] = out.reshape(NDP, SPAN, CW)

    def spread(g):
        oz = 1 - zl
        arrived(("cz", g), ss.at[g, oz, y0])
        block = ss.at[g, oz, y0]
        copy(("czp", g), block, block, yp)
        copy(("czm", g), block, block, ym)

    def spread_far(g):
        block = ss.at[g, zl, y2]
        arrived(("cf", g), block)
        copy(("czz", g), block, block, zp)

    def spread_end(g):
        oz = 1 - zl
        arrived(("cp", g), ss.at[g, zl, y3])
        arrived(("cm", g), ss.at[g, zl, y1])
        arrived(("czp", g), ss.at[g, oz, y3])
        arrived(("czm", g), ss.at[g, oz, y1])
        arrived(("czz", g), ss.at[g, oz, y2])

    factor = 1.0 / math.sqrt(2048.0)

    def gradient(g, half):
        def step(i, c):
            base = pl.multiple_of((half * 2 + i) * CW, CW)
            rows = pl.ds(base, CW)
            part = jnp.dot(
                xt[rows, :], ss[g].reshape(FEAT, CW), preferred_element_type=F32
            )
            part = (part * (pgc[rows, :] * factor)).astype(BF)
            gb[g, half, pl.ds(pl.multiple_of(i * 4, 4), 4)] = part.reshape(4, CHUNK, CW)
            return c

        lax.fori_loop(0, 2, step, 0)

    def reduce_core(g):
        gradient(g, 1 - core)
        copy(("d0", g), gb.at[g, 1 - core], dr0.at[g], cp)
        gradient(g, core)

    x0, x1, x2, x3 = xx, (xx + 1) % 4, (xx + 2) % 4, (xx + 3) % 4

    def reduce_x(g):
        arrived(("d0", g), dr0.at[g])
        hb[g] = (gb[g, core].astype(F32) + dr0[g].astype(F32)).astype(BF)
        for i, (quarter, dev) in enumerate(((x2, xf), (x1, xp), (x3, xm))):
            for k in range(2):
                copy(("x", g, i, k), hb.at[g, 4 * k + quarter], xr.at[g, i, k], dev)

    def d_copy(g, k):
        return pltpu.make_async_remote_copy(
            src_ref=rb.at[g, k],
            dst_ref=fr.at[g, zh],
            send_sem=dsend.at[g * 2 + k],
            recv_sem=drecv.at[g * 2 + zh],
            device_id=fin(k),
            device_id_type=MESH,
        )

    def to_owner(g):
        for k in range(2):
            whole = hb[g, 4 * k + x0].astype(F32)
            for i in range(3):
                arrived(("x", g, i, k), xr.at[g, i, k])
                whole = whole + xr[g, i, k].astype(F32)
            rb[g, k] = whole.astype(BF)
        for k in range(2):

            @pl.when(fin_self(k))
            def _():
                fr[g, zh] = rb[g, k]

            @pl.when(jnp.logical_not(fin_self(k)))
            def _():
                d_copy(g, k).start()

    def finish_waits(g):
        for s in range(2):

            @pl.when(jnp.logical_not(jnp.logical_and(origin, zh == s)))
            def _():
                pltpu.make_async_remote_copy(
                    src_ref=fr.at[g, s],
                    dst_ref=fr.at[g, s],
                    send_sem=dsend.at[g * 2],
                    recv_sem=drecv.at[g * 2 + s],
                    device_id=cp,
                    device_id_type=MESH,
                ).wait_recv()

    def finish(g):
        finish_waits(g)
        gw_ref[:, g * CW : (g + 1) * CW] = fr[g, 0].astype(F32) + fr[g, 1].astype(F32)

    def f_copy(peer):
        return pltpu.make_async_remote_copy(
            src_ref=pvs.at[peer],
            dst_ref=pvr.at[d],
            send_sem=fsend.at[peer],
            recv_sem=frecv.at[d],
            device_id=at(peer, t),
            device_id_type=MESH,
        )

    def f_start(i, c):
        f_copy((d + i) % NDP).start()
        return c

    def f_wait(i, c):
        p = (d + i) % NDP
        pltpu.make_async_remote_copy(
            src_ref=pvr.at[p],
            dst_ref=pvr.at[p],
            send_sem=fsend.at[p],
            recv_sem=frecv.at[p],
            device_id=at(p, t),
            device_id_type=MESH,
        ).wait_recv()
        return c

    lax.fori_loop(1, NDP, e_start, 0)
    second(0)
    def turn(i, c):
        cols = pl.ds(pl.multiple_of(i * CW, CW), CW)
        xt[cols, :] = x[:, cols].T
        return c

    lax.fori_loop(0, 4, turn, 0)
    row = lax.broadcasted_iota(jnp.int32, (RB, 1), 0)
    slot = jnp.zeros((RB, 1), jnp.int32)
    length = jnp.ones((RB, 1), F32)
    advantage = jnp.zeros((RB, 1), F32)
    first = jnp.int32(0)
    for s in range(16):
        n = len_ref[0, 0, s]
        inside = jnp.logical_and(row >= first, row < first + n)
        slot = jnp.where(inside, row - first + bin_ref[0, 0, s] * SPAN, slot)
        length = jnp.where(inside, n.astype(F32), length)
        advantage = jnp.where(inside, adv_ref[0, 0, s], advantage)
        first = first + n
    importance = jnp.minimum(jnp.exp(to_col(gap_ref[...])), 2.0)
    coef_adv = (advantage * importance / length).astype(BF).astype(F32)
    coef_pull = (BETA / length).astype(BF).astype(F32)
    pick = (
        jnp.broadcast_to(slot, (RB, NDP * SPAN))
        == lax.broadcasted_iota(jnp.int32, (RB, NDP * SPAN), 1)
    ).astype(BF)
    slot_row = to_row(slot.astype(F32))
    place = (
        lax.broadcasted_iota(jnp.int32, (NDP * SPAN, RB), 0).astype(F32)
        == jnp.broadcast_to(slot_row, (NDP * SPAN, RB))
    ).astype(BF)

    w_share(0)
    policy(0)
    start(2)
    third(0)
    second(1)
    w_share(1)
    policy(1)
    start(3)
    second(2)
    finish_unit(0)
    third(1)
    third(2)

    def p_wait(i, c):
        p = (t + i) % 8
        pltpu.make_async_remote_copy(
            src_ref=pow_r.at[p],
            dst_ref=pow_r.at[p],
            send_sem=psend.at[p],
            recv_sem=precv.at[p],
            device_id=at(d, p),
            device_id_type=MESH,
        ).wait_recv()
        return c

    lax.fori_loop(1, 8, p_wait, 0)
    power = pow_r[0]
    for k in range(1, 8):
        power = power + pow_r[k]
    scale = to_col(lax.rsqrt(power[0:1, :] * (1.0 / WIDTH) + EPS))

    second(3)

    ld_cot.wait()

    def e_wait(i, c):
        p = (d + i) % NDP
        pltpu.make_async_remote_copy(
            src_ref=cr.at[p],
            dst_ref=cr.at[p],
            send_sem=esend.at[p],
            recv_sem=erecv.at[p],
            device_id=at(p, t),
            device_id_type=MESH,
        ).wait_recv()
        return c

    lax.fori_loop(1, NDP, e_wait, 0)

    finish_unit(2)
    slopes(0)
    finish_unit(1)
    spread(0)
    third(3)
    finish_unit(3)
    slopes(1)
    spread_far(0)
    spread(1)
    spread_end(0)
    reduce_core(0)
    spread_far(1)
    reduce_x(0)
    pvr[d] = pvs[d]
    lax.fori_loop(1, NDP, f_start, 0)
    spread_end(1)
    reduce_core(1)
    to_owner(0)
    reduce_x(1)
    to_owner(1)
    lax.fori_loop(1, NDP, f_wait, 0)
    pv_ref[0, 0] = pvr[...].reshape(NDP * SPAN, VW)
    finish(0)
    finish(1)

    for c in sent:
        c.wait_send()

    w_sent(0)
    w_sent(1)

    def p_done(i, c):
        p_copy((t + i) % 8).wait_send()
        return c

    def ef_done(i, c):
        e_copy((d + i) % NDP).wait_send()
        f_copy((d + i) % NDP).wait_send()
        return c

    lax.fori_loop(1, 8, p_done, 0)
    lax.fori_loop(1, NDP, ef_done, 0)
    for g in range(NG):
        for k in range(2):

            @pl.when(jnp.logical_not(fin_self(k)))
            def _():
                d_copy(g, k).wait_send()


def hand_over(packed_ref, grads_ref, pv_ref, gw_ref):
    pv_ref[...] = packed_ref[...]
    gw_ref[...] = grads_ref[...]


def on_device(
    tokens,
    ref_gain,
    ref_weight,
    pol_gain,
    pol_weight,
    lengths,
    bins,
    advantage,
    logprob_gap,
    cotangent,
):
    any_spec = pl.BlockSpec(memory_space=pl.ANY)
    vmem = pl.BlockSpec(memory_space=pltpu.VMEM)
    smem = pl.BlockSpec(memory_space=pltpu.SMEM)
    dma = pltpu.SemaphoreType.DMA

    def buf(*shape, dtype=BF):
        return pltpu.VMEM(shape, dtype)

    packed, grads = pl.pallas_call(
        kernel,
        out_shape=(
            jax.ShapeDtypeStruct(cotangent.shape, BF),
            jax.ShapeDtypeStruct((CHUNK, VW), F32),
        ),
        in_specs=[any_spec] * 4 + [vmem, vmem, smem, smem, smem, vmem],
        out_specs=(vmem, vmem),
        scratch_shapes=[
            buf(1024, FEAT),
            buf(FEAT, 1024),
            buf(FEAT, VW),
            buf(NG, FEAT, CW),
            buf(512, VW),
            buf(NG, FEAT, CW),
            buf(NG, FEAT, CW),
            buf(FEAT, 1, dtype=F32),
            buf(4, 2, 4, RB, CW),
            buf(4, 2, 2, HB, CW),
            buf(4, 2, 2, HB, CW),
            buf(4, 2, 2, HB, CW),
            buf(4, 3, 2, RB, CW),
            buf(4, 2, 2, HB, CW),
            buf(4, RB, CW),
            buf(4, RB, CW),
            buf(4, RB, CW, dtype=F32),
            buf(4, 4, RB, CW),
            buf(4, 4, RB, CW),
            buf(4, 2, HB, CW),
            buf(4, 2, HB, CW),
            buf(4, 2, HB, CW),
            buf(4, 2, HB, CW),
            buf(RB, VW, dtype=F32),
            buf(RB, VW, dtype=F32),
            buf(8, 8, RB, dtype=F32),
            buf(8, 8, RB, dtype=F32),
            buf(NDP, SPAN, VW),
            buf(NG, 2, 4, RB, CW),
            buf(NG, 2, 8, CHUNK, CW),
            buf(NG, 8, CHUNK, CW),
            buf(NG, 8, CHUNK, CW),
            buf(NG, 3, 2, CHUNK, CW),
            buf(NG, 2, CHUNK, CW),
            buf(NG, 2, CHUNK, CW),
            buf(NDP, SPAN, VW),
            buf(NDP, SPAN, VW),
            dma((4,)),
            dma((96,)),
            dma((96,)),
            dma((NG * 8,)),
            dma((NG * 8,)),
            dma((8,)),
            dma((8,)),
            dma((NDP,)),
            dma((NDP,)),
            dma((NDP,)),
            dma((NDP,)),
            dma((4,)),
            dma((4,)),
        ],
        compiler_params=pltpu.CompilerParams(collective_id=0, has_side_effects=True),
    )(
        tokens,
        ref_weight,
        pol_weight,
        cotangent,
        ref_gain.reshape(8, RB),
        pol_gain.reshape(8, 8, RB),
        lengths,
        bins,
        advantage,
        logprob_gap.reshape(1, RB),
    )
    return pl.pallas_call(
        hand_over,
        out_shape=(
            jax.ShapeDtypeStruct(cotangent.shape, BF),
            jax.ShapeDtypeStruct((CHUNK, VW), F32),
        ),
        in_specs=[vmem, vmem],
        out_specs=(vmem, vmem),
    )(packed, grads)


def solution(mesh):
    in_specs = (
        P("dp", "tensor"),
        P("tensor"),
        P("tensor", None),
        P(),
        P("dp", None),
        P("dp", "tensor", None),
        P("dp", "tensor", None),
        P("dp", "tensor", None),
        P(("dp", "tensor")),
        P("dp", "tensor", None, None),
    )
    out_specs = (P("dp", "tensor", None, None), P(("dp", "tensor"), None))
    return jax.shard_map(
        on_device, mesh=mesh, in_specs=in_specs, out_specs=out_specs, check_vma=False
    )
```

```python
import math

import jax
import jax.numpy as jnp
from jax import lax
from jax.experimental import pallas as pl
from jax.experimental.pallas import tpu as pltpu
from jax.sharding import PartitionSpec as P

EPS = 1e-06
BETA = 1.0
MESH = pl.DeviceIdType.MESH
BF = jnp.bfloat16
F32 = jnp.float32

FEAT = 1024
RB = 128
HB = RB // 2
VW = 512
CW = 256
NG = VW // CW
WIDTH = 8192
NDP = 16
SPAN = 16
AP = 64
MODES = "ezee"
CHUNK = 64


def kernel(
    x_hbm,
    rw_hbm,
    pw_hbm,
    cot_hbm,
    rg_ref,
    pg_ref,
    len_ref,
    bin_ref,
    adv_ref,
    gap_ref,
    pv_ref,
    gw_ref,
    x,
    xt,
    wr,
    wrs,
    pw,
    wp,
    wps,
    pgc,
    pb,
    ry1,
    ryd,
    ryc,
    re,
    ycb,
    qs,
    rz,
    tq,
    z1r,
    sb,
    zr1,
    zrd,
    zrc,
    zcb,
    tref,
    tpol,
    pow_s,
    pow_r,
    cr,
    ss,
    gb,
    dr0,
    hb,
    xr,
    rb,
    fr,
    pvs,
    pvr,
    loc,
    msend,
    mrecv,
    asend,
    arecv,
    psend,
    precv,
    esend,
    erecv,
    fsend,
    frecv,
    dsend,
    drecv,
):
    d = lax.axis_index("dp")
    t = lax.axis_index("tensor")
    core = d % 2
    xx = (d // 2) % 4
    zh = d // 8
    yy = t % 4
    zl = t // 4

    def at(dd, tt):
        return (dd, tt)

    yp = at(d, zl * 4 + (yy + 1) % 4)
    ym = at(d, zl * 4 + (yy + 3) % 4)
    yf = at(d, zl * 4 + (yy + 2) % 4)
    zp = at(d, (1 - zl) * 4 + yy)
    xp = at((zh * 4 + (xx + 1) % 4) * 2 + core, t)
    xm = at((zh * 4 + (xx + 3) % 4) * 2 + core, t)
    xf = at((zh * 4 + (xx + 2) % 4) * 2 + core, t)
    cp = at(d + 1 - 2 * core, t)
    same_z = zh == zl
    origin = jnp.logical_and(xx == yy, same_z)
    dfin = (zl * 4 + yy) * 2 + core

    def fin(k):
        return at(dfin, k * 4 + xx)

    def fin_src(s):
        return at((s * 4 + yy) * 2 + core, zh * 4 + xx)

    def fin_self(k):
        return jnp.logical_and(origin, zl == k)

    ld_rw = pltpu.make_async_copy(rw_hbm, wr, loc.at[0])
    ld_x = pltpu.make_async_copy(x_hbm, x, loc.at[1])
    ld_pw = pltpu.make_async_copy(pw_hbm, pw, loc.at[2])
    ld_cot = pltpu.make_async_copy(
        cot_hbm.at[0, 0, pl.ds(pl.multiple_of(d * SPAN, SPAN), SPAN), :], cr.at[d], loc.at[3]
    )

    bar = pltpu.get_barrier_semaphore()

    def greet(dev):
        pl.semaphore_signal(bar, inc=1, device_id=dev, device_id_type=MESH)

    def greet_t(i, c):
        greet(at(d, (t + i) % 8))
        return c

    def greet_d(i, c):
        greet(at((d + i) % NDP, t))
        return c


    def greet_w(i, c):
        @pl.when(jnp.logical_or(d // 2 != t, i != t))
        def _():
            greet(at(2 * t + core, i))

        return c

    lax.fori_loop(0, 8, greet_w, 0, unroll=True)

    for s in range(2):

        @pl.when(jnp.logical_not(jnp.logical_and(origin, zh == s)))
        def _():
            greet(fin_src(s))

    lax.fori_loop(1, 8, greet_t, 0, unroll=True)
    lax.fori_loop(1, NDP, greet_d, 0, unroll=True)
    ld_rw.start()
    ld_x.start()
    ld_pw.start()
    ld_cot.start()

    eye = lax.broadcasted_iota(jnp.int32, (RB, RB), 0) == lax.broadcasted_iota(
        jnp.int32, (RB, RB), 1
    )

    def to_col(row):
        return jnp.sum(
            jnp.where(eye, jnp.broadcast_to(row, (RB, RB)), 0.0), axis=1, keepdims=True
        )

    def to_row(col):
        return jnp.sum(
            jnp.where(eye, jnp.broadcast_to(col, (RB, RB)), 0.0), axis=0, keepdims=True
        )

    ld_rw.wait()
    for b in range(8):
        rows = slice(b * RB, (b + 1) * RB)
        gcol = to_col(rg_ref[b : b + 1, :])
        for g in range(NG):
            wrs[g, rows, :] = (wr[rows, g * CW : (g + 1) * CW].astype(F32) * gcol).astype(BF)
        pgc[rows, :] = to_col(pg_ref[t, b : b + 1, :])

    ld_x.wait()

    def products(u, weight):
        def step(i, c):
            rows = pl.ds(pl.multiple_of(i * CW, CW), CW)
            part = jnp.dot(x[rows, :], weight[...], preferred_element_type=F32).astype(BF)
            pb[u, i // 2, (i % 2) * 2] = part[:RB]
            pb[u, i // 2, (i % 2) * 2 + 1] = part[RB:]
            return c

        lax.fori_loop(0, 4, step, 0)

    sent = []
    ids = {}

    def copy(name, src, dst, dev):
        n = ids.setdefault(name, len(ids))
        c = pltpu.make_async_remote_copy(
            src_ref=src,
            dst_ref=dst,
            send_sem=msend.at[n],
            recv_sem=mrecv.at[n],
            device_id=dev,
            device_id_type=MESH,
        )
        c.start()
        sent.append(c)

    def arrived(name, landed):
        n = ids[name]
        pltpu.make_async_remote_copy(
            src_ref=landed,
            dst_ref=landed,
            send_sem=msend.at[n],
            recv_sem=mrecv.at[n],
            device_id=cp,
            device_id_type=MESH,
        ).wait_recv()

    y0, y1, y2, y3 = yy, (yy + 1) % 4, (yy + 2) % 4, (yy + 3) % 4

    def start_y(u):
        n = u
        copy(("y1", u, 0), pb.at[u, :, y2, 0:HB, :], ry1.at[n, 0], yp)
        copy(("y1", u, 1), pb.at[u, :, y2, HB:RB, :], ry1.at[n, 1], ym)
        copy(("yd", u, 0), pb.at[u, :, y1, HB:RB, :], ryd.at[n, 0], yp)
        copy(("yd", u, 1), pb.at[u, :, y3, 0:HB, :], ryd.at[n, 1], ym)

    def combine_y(u):
        n = u
        arrived(("y1", u, 0), ry1.at[n, 0])
        ycb[n, 0] = (pb[u, :, y1, 0:HB, :].astype(F32) + ry1[n, 0].astype(F32)).astype(BF)
        copy(("yc", u, 0), ycb.at[n, 0], ryc.at[n, 0], yp)
        arrived(("y1", u, 1), ry1.at[n, 1])
        ycb[n, 1] = (pb[u, :, y3, HB:RB, :].astype(F32) + ry1[n, 1].astype(F32)).astype(BF)
        copy(("yc", u, 1), ycb.at[n, 1], ryc.at[n, 1], ym)

    def cross_y(u):
        n = u
        for i in range(2):
            arrived(("yd", u, i), ryd.at[n, i])
        for i in range(2):
            arrived(("yc", u, i), ryc.at[n, i])

        def part(zt, lo):
            own = pb[u, zt, y0, lo : lo + HB, :].astype(F32)
            if lo == 0:
                return own + ryc[n, 0, zt].astype(F32) + ryd[n, 1, zt].astype(F32)
            return own + ryd[n, 0, zt].astype(F32) + ryc[n, 1, zt].astype(F32)

        qs[n, 0:HB, :] = part(1 - zl, 0).astype(BF)
        qs[n, HB:RB, :] = part(1 - zl, HB).astype(BF)
        copy(("yz", u), qs.at[n], rz.at[n], zp)
        tq[n, 0:HB, :] = part(zl, 0)
        tq[n, HB:RB, :] = part(zl, HB)

    def finish_y(u, total, g):
        n = u
        arrived(("yz", u), rz.at[n])
        total[:, g * CW : (g + 1) * CW] = tq[n] + rz[n].astype(F32)

    def start_z(u):
        n = u
        for o in (2, 1, 3, 0):
            copy(("z1", u, o), pb.at[u, 1 - zl, (yy + o) % 4], z1r.at[n, o], zp)

    def sum_z(u):
        n = u
        for o in (2, 1, 3):
            arrived(("z1", u, o), z1r.at[n, o])
            sb[n, o] = (pb[u, zl, (yy + o) % 4].astype(F32) + z1r[n, o].astype(F32)).astype(BF)
            if o == 2:
                copy(("zr", u, 0), sb.at[n, 2, 0:HB, :], zr1.at[n, 0], yp)
                copy(("zr", u, 1), sb.at[n, 2, HB:RB, :], zr1.at[n, 1], ym)
            elif o == 1:
                copy(("zd", u, 0), sb.at[n, 1, HB:RB, :], zrd.at[n, 0], yp)
            else:
                copy(("zd", u, 1), sb.at[n, 3, 0:HB, :], zrd.at[n, 1], ym)

    def combine_z(u):
        n = u
        arrived(("zr", u, 0), zr1.at[n, 0])
        zcb[n, 0] = (sb[n, 1, 0:HB, :].astype(F32) + zr1[n, 0].astype(F32)).astype(BF)
        copy(("zc", u, 0), zcb.at[n, 0], zrc.at[n, 0], yp)
        arrived(("zr", u, 1), zr1.at[n, 1])
        zcb[n, 1] = (sb[n, 3, HB:RB, :].astype(F32) + zr1[n, 1].astype(F32)).astype(BF)
        copy(("zc", u, 1), zcb.at[n, 1], zrc.at[n, 1], ym)

    def finish_z(u, total, g):
        n = u
        arrived(("z1", u, 0), z1r.at[n, 0])
        for i in range(2):
            arrived(("zd", u, i), zrd.at[n, i])
        for i in range(2):
            arrived(("zc", u, i), zrc.at[n, i])
        cols = slice(g * CW, (g + 1) * CW)
        own = pb[u, zl, y0].astype(F32) + z1r[n, 0].astype(F32)
        total[0:HB, cols] = own[0:HB] + zrc[n, 0].astype(F32) + zrd[n, 1].astype(F32)
        total[HB:RB, cols] = own[HB:RB] + zrd[n, 0].astype(F32) + zrc[n, 1].astype(F32)

    def start_e(u):
        copy(("e", u, 2), pb.at[u, :, y2], re.at[u, 2], yf)
        copy(("e", u, 0), pb.at[u, :, y1], re.at[u, 0], yp)
        copy(("e", u, 1), pb.at[u, :, y3], re.at[u, 1], ym)

    def none(u):
        pass

    def cross_e(u):
        for i in range(3):
            arrived(("e", u, i), re.at[u, i])

        def part(zt):
            whole = pb[u, zt, y0].astype(F32)
            for i in range(3):
                whole = whole + re[u, i, zt].astype(F32)
            return whole

        qs[u] = part(1 - zl).astype(BF)
        copy(("yz", u), qs.at[u], rz.at[u], zp)
        tq[u] = part(zl)

    def unit(u):
        if MODES[u] == "e":
            return start_e, none, cross_e, finish_y
        return (start_y, combine_y, cross_y, finish_y) if MODES[u] == "y" else (start_z, sum_z, combine_z, finish_z)

    def start(u):
        unit(u)[0](u)

    def second(u):
        unit(u)[1](u)

    def third(u):
        unit(u)[2](u)

    def finish_unit(u):
        unit(u)[3](u, (tref, tref, tpol, tpol)[u], u % 2)

    def w_copy(g, i):
        rank = (d // 2 + t + i) % 8
        return pltpu.make_async_remote_copy(
            src_ref=pw.at[
                pl.ds(pl.multiple_of(t * AP, AP), AP), g * CW : (g + 1) * CW
            ],
            dst_ref=wp.at[g, pl.ds(pl.multiple_of(core * 512 + t * AP, AP), AP), :],
            send_sem=asend.at[g * 8 + rank],
            recv_sem=arecv.at[g * 8 + t],
            device_id=at(rank * 2 + core, d // 2),
            device_id_type=MESH,
        )

    def w_remote(i):
        return jnp.logical_or(d // 2 != t, (d // 2 + t + i) % 8 != d // 2)

    def w_start(g):
        def step(i, c):
            @pl.when(w_remote(i))
            def _():
                w_copy(g, i).start()

            return c

        lax.fori_loop(0, 8, step, 0)

    def w_sent(g):
        def step(i, c):
            @pl.when(w_remote(i))
            def _():
                w_copy(g, i).wait_send()

            return c

        lax.fori_loop(0, 8, step, 0)

    def w_share(g):
        def step(i, c):
            part = wp.at[g, pl.ds(pl.multiple_of(core * 512 + i * AP, AP), AP), :]

            @pl.when(jnp.logical_or(d // 2 != t, i != t))
            def _():
                pltpu.make_async_remote_copy(
                    src_ref=part,
                    dst_ref=part,
                    send_sem=asend.at[g * 8 + i],
                    recv_sem=arecv.at[g * 8 + i],
                    device_id=cp,
                    device_id_type=MESH,
                ).wait_recv()

            return c

        lax.fori_loop(0, 8, step, 0)
        mine = wp.at[g, pl.ds(pl.multiple_of(core * 512, 512), 512), :]
        copy(("w", g), mine, mine, cp)

    products(0, wrs.at[0])
    products(1, wrs.at[1])

    ld_pw.wait()

    @pl.when(d // 2 == t)
    def _():
        for g in range(NG):
            wp[g, pl.ds(pl.multiple_of(core * 512 + t * AP, AP), AP), :] = pw[
                pl.ds(pl.multiple_of(t * AP, AP), AP), g * CW : (g + 1) * CW
            ]

    pl.semaphore_wait(
        bar,
        30
        - jnp.where(d // 2 == t, 1, 0)
        + jnp.where(fin_self(0), 0, 1)
        + jnp.where(fin_self(1), 0, 1),
    )


    w_start(0)
    start(0)
    w_start(1)
    start(1)

    def squares(b, c):
        rows = pl.ds(pl.multiple_of(b * RB, RB), RB)
        xb = x[rows, :].astype(F32)
        part = jnp.sum(xb * xb, axis=1, keepdims=True)
        pow_s[b] = jnp.broadcast_to(to_row(part), (8, RB))
        return c

    lax.fori_loop(0, 8, squares, 0)
    pow_r[t] = pow_s[t]

    def p_copy(peer):
        return pltpu.make_async_remote_copy(
            src_ref=pow_s.at[peer],
            dst_ref=pow_r.at[t],
            send_sem=psend.at[peer],
            recv_sem=precv.at[t],
            device_id=at(d, peer),
            device_id_type=MESH,
        )

    def p_start(i, c):
        p_copy((t + i) % 8).start()
        return c

    lax.fori_loop(1, 8, p_start, 0, unroll=True)


    def e_copy(peer):
        return pltpu.make_async_remote_copy(
            src_ref=cot_hbm.at[0, 0, pl.ds(pl.multiple_of(peer * SPAN, SPAN), SPAN), :],
            dst_ref=cr.at[d],
            send_sem=esend.at[peer],
            recv_sem=erecv.at[d],
            device_id=at(peer, t),
            device_id_type=MESH,
        )

    def e_start(i, c):
        e_copy((d + i) % NDP).start()
        return c

    def policy(g):
        arrived(("w", g), wp.at[g, pl.ds(pl.multiple_of((1 - core) * 512, 512), 512), :])
        for b in range(8):
            rows = slice(b * RB, (b + 1) * RB)
            wps[g, rows, :] = (wp[g, rows, :].astype(F32) * pgc[rows, :]).astype(BF)
        products(2 + g, wps.at[g])

    def slopes(g):
        cols = slice(g * CW, (g + 1) * CW)
        upstream = jnp.dot(
            pick, cr[:, :, cols].reshape(NDP * SPAN, CW), preferred_element_type=F32
        )
        values = tpol[:, cols] * scale
        ref_values = (tref[:, cols] * scale).astype(BF).astype(F32)
        slope = coef_adv * upstream + coef_pull * (values - ref_values)
        ss[g, zl, y0] = (slope * scale).astype(BF)
        mine = ss.at[g, zl, y0]
        copy(("cz", g), mine, mine, zp)
        copy(("cf", g), mine, mine, yf)
        copy(("cp", g), mine, mine, yp)
        copy(("cm", g), mine, mine, ym)
        out = jnp.dot(place, values.astype(BF), preferred_element_type=F32).astype(BF)
        pvs[:, :, cols] = out.reshape(NDP, SPAN, CW)

    def spread(g):
        oz = 1 - zl
        arrived(("cz", g), ss.at[g, oz, y0])
        block = ss.at[g, oz, y0]
        copy(("czp", g), block, block, yp)
        copy(("czm", g), block, block, ym)

    def spread_far(g):
        block = ss.at[g, zl, y2]
        arrived(("cf", g), block)
        copy(("czz", g), block, block, zp)

    def spread_end(g):
        oz = 1 - zl
        arrived(("cp", g), ss.at[g, zl, y3])
        arrived(("cm", g), ss.at[g, zl, y1])
        arrived(("czp", g), ss.at[g, oz, y3])
        arrived(("czm", g), ss.at[g, oz, y1])
        arrived(("czz", g), ss.at[g, oz, y2])

    factor = 1.0 / math.sqrt(2048.0)

    def gradient(g, half):
        def step(i, c):
            base = pl.multiple_of((half * 2 + i) * CW, CW)
            rows = pl.ds(base, CW)
            part = jnp.dot(
                xt[rows, :], ss[g].reshape(FEAT, CW), preferred_element_type=F32
            )
            part = (part * (pgc[rows, :] * factor)).astype(BF)
            gb[g, half, pl.ds(pl.multiple_of(i * 4, 4), 4)] = part.reshape(4, CHUNK, CW)
            return c

        lax.fori_loop(0, 2, step, 0)

    def reduce_core(g):
        gradient(g, 1 - core)
        copy(("d0", g), gb.at[g, 1 - core], dr0.at[g], cp)
        gradient(g, core)

    x0, x1, x2, x3 = xx, (xx + 1) % 4, (xx + 2) % 4, (xx + 3) % 4

    def reduce_x(g):
        arrived(("d0", g), dr0.at[g])
        hb[g] = (gb[g, core].astype(F32) + dr0[g].astype(F32)).astype(BF)
        for i, (quarter, dev) in enumerate(((x2, xf), (x1, xp), (x3, xm))):
            for k in range(2):
                copy(("x", g, i, k), hb.at[g, 4 * k + quarter], xr.at[g, i, k], dev)

    def d_copy(g, k):
        return pltpu.make_async_remote_copy(
            src_ref=rb.at[g, k],
            dst_ref=fr.at[g, zh],
            send_sem=dsend.at[g * 2 + k],
            recv_sem=drecv.at[g * 2 + zh],
            device_id=fin(k),
            device_id_type=MESH,
        )

    def to_owner(g):
        for k in range(2):
            whole = hb[g, 4 * k + x0].astype(F32)
            for i in range(3):
                arrived(("x", g, i, k), xr.at[g, i, k])
                whole = whole + xr[g, i, k].astype(F32)
            rb[g, k] = whole.astype(BF)
        for k in range(2):

            @pl.when(fin_self(k))
            def _():
                fr[g, zh] = rb[g, k]

            @pl.when(jnp.logical_not(fin_self(k)))
            def _():
                d_copy(g, k).start()

    def finish_waits(g):
        for s in range(2):

            @pl.when(jnp.logical_not(jnp.logical_and(origin, zh == s)))
            def _():
                pltpu.make_async_remote_copy(
                    src_ref=fr.at[g, s],
                    dst_ref=fr.at[g, s],
                    send_sem=dsend.at[g * 2],
                    recv_sem=drecv.at[g * 2 + s],
                    device_id=cp,
                    device_id_type=MESH,
                ).wait_recv()

    def finish(g):
        finish_waits(g)
        gw_ref[:, g * CW : (g + 1) * CW] = fr[g, 0].astype(F32) + fr[g, 1].astype(F32)

    def f_copy(peer):
        return pltpu.make_async_remote_copy(
            src_ref=pvs.at[peer],
            dst_ref=pvr.at[d],
            send_sem=fsend.at[peer],
            recv_sem=frecv.at[d],
            device_id=at(peer, t),
            device_id_type=MESH,
        )

    def f_start(i, c):
        f_copy((d + i) % NDP).start()
        return c

    def f_wait(i, c):
        p = (d + i) % NDP
        pltpu.make_async_remote_copy(
            src_ref=pvr.at[p],
            dst_ref=pvr.at[p],
            send_sem=fsend.at[p],
            recv_sem=frecv.at[p],
            device_id=at(p, t),
            device_id_type=MESH,
        ).wait_recv()
        return c

    lax.fori_loop(1, NDP, e_start, 0, unroll=True)
    second(0)
    def turn(i, c):
        cols = pl.ds(pl.multiple_of(i * CW, CW), CW)
        xt[cols, :] = x[:, cols].T
        return c

    lax.fori_loop(0, 4, turn, 0)
    row = lax.broadcasted_iota(jnp.int32, (RB, 1), 0)
    slot = jnp.zeros((RB, 1), jnp.int32)
    length = jnp.ones((RB, 1), F32)
    advantage = jnp.zeros((RB, 1), F32)
    first = jnp.int32(0)
    for s in range(16):
        n = len_ref[0, 0, s]
        inside = jnp.logical_and(row >= first, row < first + n)
        slot = jnp.where(inside, row - first + bin_ref[0, 0, s] * SPAN, slot)
        length = jnp.where(inside, n.astype(F32), length)
        advantage = jnp.where(inside, adv_ref[0, 0, s], advantage)
        first = first + n
    importance = jnp.minimum(jnp.exp(to_col(gap_ref[...])), 2.0)
    coef_adv = (advantage * importance / length).astype(BF).astype(F32)
    coef_pull = (BETA / length).astype(BF).astype(F32)
    pick = (
        jnp.broadcast_to(slot, (RB, NDP * SPAN))
        == lax.broadcasted_iota(jnp.int32, (RB, NDP * SPAN), 1)
    ).astype(BF)
    slot_row = to_row(slot.astype(F32))
    place = (
        lax.broadcasted_iota(jnp.int32, (NDP * SPAN, RB), 0).astype(F32)
        == jnp.broadcast_to(slot_row, (NDP * SPAN, RB))
    ).astype(BF)

    w_share(0)
    policy(0)
    start(2)
    third(0)
    second(1)
    w_share(1)
    policy(1)
    start(3)
    second(2)
    finish_unit(0)
    third(1)
    third(2)

    def p_wait(i, c):
        p = (t + i) % 8
        pltpu.make_async_remote_copy(
            src_ref=pow_r.at[p],
            dst_ref=pow_r.at[p],
            send_sem=psend.at[p],
            recv_sem=precv.at[p],
            device_id=at(d, p),
            device_id_type=MESH,
        ).wait_recv()
        return c

    lax.fori_loop(1, 8, p_wait, 0)
    power = pow_r[0]
    for k in range(1, 8):
        power = power + pow_r[k]
    scale = to_col(lax.rsqrt(power[0:1, :] * (1.0 / WIDTH) + EPS))

    second(3)

    ld_cot.wait()

    def e_wait(i, c):
        p = (d + i) % NDP
        pltpu.make_async_remote_copy(
            src_ref=cr.at[p],
            dst_ref=cr.at[p],
            send_sem=esend.at[p],
            recv_sem=erecv.at[p],
            device_id=at(p, t),
            device_id_type=MESH,
        ).wait_recv()
        return c

    lax.fori_loop(1, NDP, e_wait, 0)

    finish_unit(2)
    slopes(0)
    finish_unit(1)
    spread(0)
    third(3)
    finish_unit(3)
    slopes(1)
    spread_far(0)
    spread(1)
    spread_end(0)
    reduce_core(0)
    spread_far(1)
    reduce_x(0)
    pvr[d] = pvs[d]
    lax.fori_loop(1, NDP, f_start, 0, unroll=True)
    spread_end(1)
    reduce_core(1)
    to_owner(0)
    reduce_x(1)
    to_owner(1)
    lax.fori_loop(1, NDP, f_wait, 0)
    pv_ref[0, 0] = pvr[...].reshape(NDP * SPAN, VW)
    finish(0)
    finish(1)

    for c in sent:
        c.wait_send()

    w_sent(0)
    w_sent(1)

    def p_done(i, c):
        p_copy((t + i) % 8).wait_send()
        return c

    def ef_done(i, c):
        e_copy((d + i) % NDP).wait_send()
        f_copy((d + i) % NDP).wait_send()
        return c

    lax.fori_loop(1, 8, p_done, 0)
    lax.fori_loop(1, NDP, ef_done, 0)
    for g in range(NG):
        for k in range(2):

            @pl.when(jnp.logical_not(fin_self(k)))
            def _():
                d_copy(g, k).wait_send()


def hand_over(packed_ref, grads_ref, pv_ref, gw_ref):
    pv_ref[...] = packed_ref[...]
    gw_ref[...] = grads_ref[...]


def on_device(
    tokens,
    ref_gain,
    ref_weight,
    pol_gain,
    pol_weight,
    lengths,
    bins,
    advantage,
    logprob_gap,
    cotangent,
):
    any_spec = pl.BlockSpec(memory_space=pl.ANY)
    vmem = pl.BlockSpec(memory_space=pltpu.VMEM)
    smem = pl.BlockSpec(memory_space=pltpu.SMEM)
    dma = pltpu.SemaphoreType.DMA

    def buf(*shape, dtype=BF):
        return pltpu.VMEM(shape, dtype)

    packed, grads = pl.pallas_call(
        kernel,
        out_shape=(
            jax.ShapeDtypeStruct(cotangent.shape, BF),
            jax.ShapeDtypeStruct((CHUNK, VW), F32),
        ),
        in_specs=[any_spec] * 4 + [vmem, vmem, smem, smem, smem, vmem],
        out_specs=(vmem, vmem),
        scratch_shapes=[
            buf(1024, FEAT),
            buf(FEAT, 1024),
            buf(FEAT, VW),
            buf(NG, FEAT, CW),
            buf(512, VW),
            buf(NG, FEAT, CW),
            buf(NG, FEAT, CW),
            buf(FEAT, 1, dtype=F32),
            buf(4, 2, 4, RB, CW),
            buf(4, 2, 2, HB, CW),
            buf(4, 2, 2, HB, CW),
            buf(4, 2, 2, HB, CW),
            buf(4, 3, 2, RB, CW),
            buf(4, 2, 2, HB, CW),
            buf(4, RB, CW),
            buf(4, RB, CW),
            buf(4, RB, CW, dtype=F32),
            buf(4, 4, RB, CW),
            buf(4, 4, RB, CW),
            buf(4, 2, HB, CW),
            buf(4, 2, HB, CW),
            buf(4, 2, HB, CW),
            buf(4, 2, HB, CW),
            buf(RB, VW, dtype=F32),
            buf(RB, VW, dtype=F32),
            buf(8, 8, RB, dtype=F32),
            buf(8, 8, RB, dtype=F32),
            buf(NDP, SPAN, VW),
            buf(NG, 2, 4, RB, CW),
            buf(NG, 2, 8, CHUNK, CW),
            buf(NG, 8, CHUNK, CW),
            buf(NG, 8, CHUNK, CW),
            buf(NG, 3, 2, CHUNK, CW),
            buf(NG, 2, CHUNK, CW),
            buf(NG, 2, CHUNK, CW),
            buf(NDP, SPAN, VW),
            buf(NDP, SPAN, VW),
            dma((4,)),
            dma((96,)),
            dma((96,)),
            dma((NG * 8,)),
            dma((NG * 8,)),
            dma((8,)),
            dma((8,)),
            dma((NDP,)),
            dma((NDP,)),
            dma((NDP,)),
            dma((NDP,)),
            dma((4,)),
            dma((4,)),
        ],
        compiler_params=pltpu.CompilerParams(collective_id=0, has_side_effects=True),
    )(
        tokens,
        ref_weight,
        pol_weight,
        cotangent,
        ref_gain.reshape(8, RB),
        pol_gain.reshape(8, 8, RB),
        lengths,
        bins,
        advantage,
        logprob_gap.reshape(1, RB),
    )
    return pl.pallas_call(
        hand_over,
        out_shape=(
            jax.ShapeDtypeStruct(cotangent.shape, BF),
            jax.ShapeDtypeStruct((CHUNK, VW), F32),
        ),
        in_specs=[vmem, vmem],
        out_specs=(vmem, vmem),
    )(packed, grads)


def solution(mesh):
    in_specs = (
        P("dp", "tensor"),
        P("tensor"),
        P("tensor", None),
        P(),
        P("dp", None),
        P("dp", "tensor", None),
        P("dp", "tensor", None),
        P("dp", "tensor", None),
        P(("dp", "tensor")),
        P("dp", "tensor", None, None),
    )
    out_specs = (P("dp", "tensor", None, None), P(("dp", "tensor"), None))
    return jax.shard_map(
        on_device, mesh=mesh, in_specs=in_specs, out_specs=out_specs, check_vma=False
    )
```

```python
import math

import jax
import jax.numpy as jnp
from jax import lax
from jax.experimental import pallas as pl
from jax.experimental.pallas import tpu as pltpu
from jax.sharding import PartitionSpec as P

EPS = 1e-06
BETA = 1.0
MESH = pl.DeviceIdType.MESH
BF = jnp.bfloat16
F32 = jnp.float32

FEAT = 1024
RB = 128
HB = RB // 2
VW = 512
CW = 256
NG = VW // CW
WIDTH = 8192
NDP = 16
SPAN = 16
AP = 64
MODES = "ezee"
CHUNK = 64


def kernel(
    x_hbm,
    rw_hbm,
    pw_hbm,
    cot_hbm,
    rg_ref,
    pg_ref,
    len_ref,
    bin_ref,
    adv_ref,
    gap_ref,
    pv_ref,
    gw_ref,
    x,
    xt,
    wr,
    wrs,
    pw,
    wp,
    wps,
    pgc,
    pb,
    ry1,
    ryd,
    ryc,
    re,
    ycb,
    qs,
    rz,
    tq,
    z1r,
    sb,
    zr1,
    zrd,
    zrc,
    zcb,
    tref,
    tpol,
    pow_s,
    pow_r,
    cr,
    ss,
    gb,
    dr0,
    hb,
    xr,
    rb,
    fr,
    pvs,
    pvr,
    loc,
    msend,
    mrecv,
    asend,
    arecv,
    psend,
    precv,
    esend,
    erecv,
    fsend,
    frecv,
    dsend,
    drecv,
):
    d = lax.axis_index("dp")
    t = lax.axis_index("tensor")
    core = d % 2
    xx = (d // 2) % 4
    zh = d // 8
    yy = t % 4
    zl = t // 4

    def at(dd, tt):
        return (dd, tt)

    yp = at(d, zl * 4 + (yy + 1) % 4)
    ym = at(d, zl * 4 + (yy + 3) % 4)
    yf = at(d, zl * 4 + (yy + 2) % 4)
    zp = at(d, (1 - zl) * 4 + yy)
    xp = at((zh * 4 + (xx + 1) % 4) * 2 + core, t)
    xm = at((zh * 4 + (xx + 3) % 4) * 2 + core, t)
    xf = at((zh * 4 + (xx + 2) % 4) * 2 + core, t)
    cp = at(d + 1 - 2 * core, t)
    same_z = zh == zl
    origin = jnp.logical_and(xx == yy, same_z)
    dfin = (zl * 4 + yy) * 2 + core

    def fin(k):
        return at(dfin, k * 4 + xx)

    def fin_src(s):
        return at((s * 4 + yy) * 2 + core, zh * 4 + xx)

    def fin_self(k):
        return jnp.logical_and(origin, zl == k)

    ld_rw = pltpu.make_async_copy(rw_hbm, wr, loc.at[0])
    ld_x = pltpu.make_async_copy(x_hbm, x, loc.at[1])
    ld_pw = pltpu.make_async_copy(pw_hbm, pw, loc.at[2])
    ld_cot = pltpu.make_async_copy(
        cot_hbm.at[0, 0, pl.ds(pl.multiple_of(d * SPAN, SPAN), SPAN), :], cr.at[d], loc.at[3]
    )

    bar = pltpu.get_barrier_semaphore()

    def greet(dev):
        pl.semaphore_signal(bar, inc=1, device_id=dev, device_id_type=MESH)

    def greet_t(i, c):
        greet(at(d, (t + i) % 8))
        return c

    def greet_d(i, c):
        greet(at((d + i) % NDP, t))
        return c


    def greet_w(i, c):
        @pl.when(jnp.logical_or(d // 2 != t, i != t))
        def _():
            greet(at(2 * t + core, i))

        return c

    lax.fori_loop(0, 8, greet_w, 0, unroll=True)

    for s in range(2):

        @pl.when(jnp.logical_not(jnp.logical_and(origin, zh == s)))
        def _():
            greet(fin_src(s))

    lax.fori_loop(1, 8, greet_t, 0, unroll=True)
    lax.fori_loop(1, NDP, greet_d, 0, unroll=True)
    ld_rw.start()
    ld_x.start()
    ld_pw.start()
    ld_cot.start()

    eye = lax.broadcasted_iota(jnp.int32, (RB, RB), 0) == lax.broadcasted_iota(
        jnp.int32, (RB, RB), 1
    )

    def to_col(row):
        return jnp.sum(
            jnp.where(eye, jnp.broadcast_to(row, (RB, RB)), 0.0), axis=1, keepdims=True
        )

    def to_row(col):
        return jnp.sum(
            jnp.where(eye, jnp.broadcast_to(col, (RB, RB)), 0.0), axis=0, keepdims=True
        )

    ld_rw.wait()
    for b in range(8):
        rows = slice(b * RB, (b + 1) * RB)
        gcol = to_col(rg_ref[b : b + 1, :])
        for g in range(NG):
            wrs[g, rows, :] = (wr[rows, g * CW : (g + 1) * CW].astype(F32) * gcol).astype(BF)
        pgc[rows, :] = to_col(pg_ref[t, b : b + 1, :])

    ld_x.wait()

    def products(u, weight):
        def step(i, c):
            rows = pl.ds(pl.multiple_of(i * CW, CW), CW)
            part = jnp.dot(x[rows, :], weight[...], preferred_element_type=F32).astype(BF)
            pb[u, i // 2, (i % 2) * 2] = part[:RB]
            pb[u, i // 2, (i % 2) * 2 + 1] = part[RB:]
            return c

        lax.fori_loop(0, 4, step, 0)

    sent = []
    ids = {}

    def copy(name, src, dst, dev):
        n = ids.setdefault(name, len(ids))
        c = pltpu.make_async_remote_copy(
            src_ref=src,
            dst_ref=dst,
            send_sem=msend.at[n],
            recv_sem=mrecv.at[n],
            device_id=dev,
            device_id_type=MESH,
        )
        c.start()
        sent.append(c)

    def arrived(name, landed):
        n = ids[name]
        pltpu.make_async_remote_copy(
            src_ref=landed,
            dst_ref=landed,
            send_sem=msend.at[n],
            recv_sem=mrecv.at[n],
            device_id=cp,
            device_id_type=MESH,
        ).wait_recv()

    y0, y1, y2, y3 = yy, (yy + 1) % 4, (yy + 2) % 4, (yy + 3) % 4

    def start_y(u):
        n = u
        copy(("y1", u, 0), pb.at[u, :, y2, 0:HB, :], ry1.at[n, 0], yp)
        copy(("y1", u, 1), pb.at[u, :, y2, HB:RB, :], ry1.at[n, 1], ym)
        copy(("yd", u, 0), pb.at[u, :, y1, HB:RB, :], ryd.at[n, 0], yp)
        copy(("yd", u, 1), pb.at[u, :, y3, 0:HB, :], ryd.at[n, 1], ym)

    def combine_y(u):
        n = u
        arrived(("y1", u, 0), ry1.at[n, 0])
        ycb[n, 0] = (pb[u, :, y1, 0:HB, :].astype(F32) + ry1[n, 0].astype(F32)).astype(BF)
        copy(("yc", u, 0), ycb.at[n, 0], ryc.at[n, 0], yp)
        arrived(("y1", u, 1), ry1.at[n, 1])
        ycb[n, 1] = (pb[u, :, y3, HB:RB, :].astype(F32) + ry1[n, 1].astype(F32)).astype(BF)
        copy(("yc", u, 1), ycb.at[n, 1], ryc.at[n, 1], ym)

    def cross_y(u):
        n = u
        for i in range(2):
            arrived(("yd", u, i), ryd.at[n, i])
        for i in range(2):
            arrived(("yc", u, i), ryc.at[n, i])

        def part(zt, lo):
            own = pb[u, zt, y0, lo : lo + HB, :].astype(F32)
            if lo == 0:
                return own + ryc[n, 0, zt].astype(F32) + ryd[n, 1, zt].astype(F32)
            return own + ryd[n, 0, zt].astype(F32) + ryc[n, 1, zt].astype(F32)

        qs[n, 0:HB, :] = part(1 - zl, 0).astype(BF)
        qs[n, HB:RB, :] = part(1 - zl, HB).astype(BF)
        copy(("yz", u), qs.at[n], rz.at[n], zp)
        tq[n, 0:HB, :] = part(zl, 0)
        tq[n, HB:RB, :] = part(zl, HB)

    def finish_y(u, total, g):
        n = u
        arrived(("yz", u), rz.at[n])
        total[:, g * CW : (g + 1) * CW] = tq[n] + rz[n].astype(F32)

    def start_z(u):
        n = u
        for o in (2, 1, 3, 0):
            copy(("z1", u, o), pb.at[u, 1 - zl, (yy + o) % 4], z1r.at[n, o], zp)

    def sum_z(u):
        n = u
        for o in (2, 1, 3):
            arrived(("z1", u, o), z1r.at[n, o])
            sb[n, o] = (pb[u, zl, (yy + o) % 4].astype(F32) + z1r[n, o].astype(F32)).astype(BF)
            if o == 2:
                copy(("zr", u, 0), sb.at[n, 2, 0:HB, :], zr1.at[n, 0], yp)
                copy(("zr", u, 1), sb.at[n, 2, HB:RB, :], zr1.at[n, 1], ym)
            elif o == 1:
                copy(("zd", u, 0), sb.at[n, 1, HB:RB, :], zrd.at[n, 0], yp)
            else:
                copy(("zd", u, 1), sb.at[n, 3, 0:HB, :], zrd.at[n, 1], ym)

    def combine_z(u):
        n = u
        arrived(("zr", u, 0), zr1.at[n, 0])
        zcb[n, 0] = (sb[n, 1, 0:HB, :].astype(F32) + zr1[n, 0].astype(F32)).astype(BF)
        copy(("zc", u, 0), zcb.at[n, 0], zrc.at[n, 0], yp)
        arrived(("zr", u, 1), zr1.at[n, 1])
        zcb[n, 1] = (sb[n, 3, HB:RB, :].astype(F32) + zr1[n, 1].astype(F32)).astype(BF)
        copy(("zc", u, 1), zcb.at[n, 1], zrc.at[n, 1], ym)

    def finish_z(u, total, g):
        n = u
        arrived(("z1", u, 0), z1r.at[n, 0])
        for i in range(2):
            arrived(("zd", u, i), zrd.at[n, i])
        for i in range(2):
            arrived(("zc", u, i), zrc.at[n, i])
        cols = slice(g * CW, (g + 1) * CW)
        own = pb[u, zl, y0].astype(F32) + z1r[n, 0].astype(F32)
        total[0:HB, cols] = own[0:HB] + zrc[n, 0].astype(F32) + zrd[n, 1].astype(F32)
        total[HB:RB, cols] = own[HB:RB] + zrd[n, 0].astype(F32) + zrc[n, 1].astype(F32)

    def start_e(u):
        copy(("e", u, 2), pb.at[u, :, y2], re.at[u, 2], yf)
        copy(("e", u, 0), pb.at[u, :, y1], re.at[u, 0], yp)
        copy(("e", u, 1), pb.at[u, :, y3], re.at[u, 1], ym)

    def none(u):
        pass

    def cross_e(u):
        for i in range(3):
            arrived(("e", u, i), re.at[u, i])

        def part(zt):
            whole = pb[u, zt, y0].astype(F32)
            for i in range(3):
                whole = whole + re[u, i, zt].astype(F32)
            return whole

        qs[u] = part(1 - zl).astype(BF)
        copy(("yz", u), qs.at[u], rz.at[u], zp)
        tq[u] = part(zl)

    def unit(u):
        if MODES[u] == "e":
            return start_e, none, cross_e, finish_y
        return (start_y, combine_y, cross_y, finish_y) if MODES[u] == "y" else (start_z, sum_z, combine_z, finish_z)

    def start(u):
        unit(u)[0](u)

    def second(u):
        unit(u)[1](u)

    def third(u):
        unit(u)[2](u)

    def finish_unit(u):
        unit(u)[3](u, (tref, tref, tpol, tpol)[u], u % 2)

    def w_copy(g, i):
        rank = (d // 2 + t + i) % 8
        return pltpu.make_async_remote_copy(
            src_ref=pw.at[
                pl.ds(pl.multiple_of(t * AP, AP), AP), g * CW : (g + 1) * CW
            ],
            dst_ref=wp.at[g, pl.ds(pl.multiple_of(core * 512 + t * AP, AP), AP), :],
            send_sem=asend.at[g * 8 + rank],
            recv_sem=arecv.at[g * 8 + t],
            device_id=at(rank * 2 + core, d // 2),
            device_id_type=MESH,
        )

    def w_remote(i):
        return jnp.logical_or(d // 2 != t, (d // 2 + t + i) % 8 != d // 2)

    def w_start(g):
        def step(i, c):
            @pl.when(w_remote(i))
            def _():
                w_copy(g, i).start()

            return c

        lax.fori_loop(0, 8, step, 0, unroll=True)

    def w_sent(g):
        def step(i, c):
            @pl.when(w_remote(i))
            def _():
                w_copy(g, i).wait_send()

            return c

        lax.fori_loop(0, 8, step, 0)

    def w_share(g):
        def step(i, c):
            part = wp.at[g, pl.ds(pl.multiple_of(core * 512 + i * AP, AP), AP), :]

            @pl.when(jnp.logical_or(d // 2 != t, i != t))
            def _():
                pltpu.make_async_remote_copy(
                    src_ref=part,
                    dst_ref=part,
                    send_sem=asend.at[g * 8 + i],
                    recv_sem=arecv.at[g * 8 + i],
                    device_id=cp,
                    device_id_type=MESH,
                ).wait_recv()

            return c

        lax.fori_loop(0, 8, step, 0)
        mine = wp.at[g, pl.ds(pl.multiple_of(core * 512, 512), 512), :]
        copy(("w", g), mine, mine, cp)

    products(0, wrs.at[0])
    products(1, wrs.at[1])

    ld_pw.wait()

    @pl.when(d // 2 == t)
    def _():
        for g in range(NG):
            wp[g, pl.ds(pl.multiple_of(core * 512 + t * AP, AP), AP), :] = pw[
                pl.ds(pl.multiple_of(t * AP, AP), AP), g * CW : (g + 1) * CW
            ]

    pl.semaphore_wait(
        bar,
        30
        - jnp.where(d // 2 == t, 1, 0)
        + jnp.where(fin_self(0), 0, 1)
        + jnp.where(fin_self(1), 0, 1),
    )


    w_start(0)
    start(0)
    w_start(1)
    start(1)

    def squares(b, c):
        rows = pl.ds(pl.multiple_of(b * RB, RB), RB)
        xb = x[rows, :].astype(F32)
        part = jnp.sum(xb * xb, axis=1, keepdims=True)
        pow_s[b] = jnp.broadcast_to(to_row(part), (8, RB))
        return c

    lax.fori_loop(0, 8, squares, 0)
    pow_r[t] = pow_s[t]

    def p_copy(peer):
        return pltpu.make_async_remote_copy(
            src_ref=pow_s.at[peer],
            dst_ref=pow_r.at[t],
            send_sem=psend.at[peer],
            recv_sem=precv.at[t],
            device_id=at(d, peer),
            device_id_type=MESH,
        )

    def p_start(i, c):
        p_copy((t + i) % 8).start()
        return c

    lax.fori_loop(1, 8, p_start, 0, unroll=True)


    def e_copy(peer):
        return pltpu.make_async_remote_copy(
            src_ref=cot_hbm.at[0, 0, pl.ds(pl.multiple_of(peer * SPAN, SPAN), SPAN), :],
            dst_ref=cr.at[d],
            send_sem=esend.at[peer],
            recv_sem=erecv.at[d],
            device_id=at(peer, t),
            device_id_type=MESH,
        )

    def e_start(i, c):
        e_copy((d + i) % NDP).start()
        return c

    def policy(g):
        arrived(("w", g), wp.at[g, pl.ds(pl.multiple_of((1 - core) * 512, 512), 512), :])
        for b in range(8):
            rows = slice(b * RB, (b + 1) * RB)
            wps[g, rows, :] = (wp[g, rows, :].astype(F32) * pgc[rows, :]).astype(BF)
        products(2 + g, wps.at[g])

    def slopes(g):
        cols = slice(g * CW, (g + 1) * CW)
        upstream = jnp.dot(
            pick, cr[:, :, cols].reshape(NDP * SPAN, CW), preferred_element_type=F32
        )
        values = tpol[:, cols] * scale
        ref_values = (tref[:, cols] * scale).astype(BF).astype(F32)
        slope = coef_adv * upstream + coef_pull * (values - ref_values)
        ss[g, zl, y0] = (slope * scale).astype(BF)
        mine = ss.at[g, zl, y0]
        copy(("cz", g), mine, mine, zp)
        copy(("cf", g), mine, mine, yf)
        copy(("cp", g), mine, mine, yp)
        copy(("cm", g), mine, mine, ym)
        out = jnp.dot(place, values.astype(BF), preferred_element_type=F32).astype(BF)
        pvs[:, :, cols] = out.reshape(NDP, SPAN, CW)

    def spread(g):
        oz = 1 - zl
        arrived(("cz", g), ss.at[g, oz, y0])
        block = ss.at[g, oz, y0]
        copy(("czp", g), block, block, yp)
        copy(("czm", g), block, block, ym)

    def spread_far(g):
        block = ss.at[g, zl, y2]
        arrived(("cf", g), block)
        copy(("czz", g), block, block, zp)

    def spread_end(g):
        oz = 1 - zl
        arrived(("cp", g), ss.at[g, zl, y3])
        arrived(("cm", g), ss.at[g, zl, y1])
        arrived(("czp", g), ss.at[g, oz, y3])
        arrived(("czm", g), ss.at[g, oz, y1])
        arrived(("czz", g), ss.at[g, oz, y2])

    factor = 1.0 / math.sqrt(2048.0)

    def gradient(g, half):
        def step(i, c):
            base = pl.multiple_of((half * 2 + i) * CW, CW)
            rows = pl.ds(base, CW)
            part = jnp.dot(
                xt[rows, :], ss[g].reshape(FEAT, CW), preferred_element_type=F32
            )
            part = (part * (pgc[rows, :] * factor)).astype(BF)
            gb[g, half, pl.ds(pl.multiple_of(i * 4, 4), 4)] = part.reshape(4, CHUNK, CW)
            return c

        lax.fori_loop(0, 2, step, 0)

    def reduce_core(g):
        gradient(g, 1 - core)
        copy(("d0", g), gb.at[g, 1 - core], dr0.at[g], cp)
        gradient(g, core)

    x0, x1, x2, x3 = xx, (xx + 1) % 4, (xx + 2) % 4, (xx + 3) % 4

    def reduce_x(g):
        arrived(("d0", g), dr0.at[g])
        hb[g] = (gb[g, core].astype(F32) + dr0[g].astype(F32)).astype(BF)
        for i, (quarter, dev) in enumerate(((x2, xf), (x1, xp), (x3, xm))):
            for k in range(2):
                copy(("x", g, i, k), hb.at[g, 4 * k + quarter], xr.at[g, i, k], dev)

    def d_copy(g, k):
        return pltpu.make_async_remote_copy(
            src_ref=rb.at[g, k],
            dst_ref=fr.at[g, zh],
            send_sem=dsend.at[g * 2 + k],
            recv_sem=drecv.at[g * 2 + zh],
            device_id=fin(k),
            device_id_type=MESH,
        )

    def to_owner(g):
        for k in range(2):
            whole = hb[g, 4 * k + x0].astype(F32)
            for i in range(3):
                arrived(("x", g, i, k), xr.at[g, i, k])
                whole = whole + xr[g, i, k].astype(F32)
            rb[g, k] = whole.astype(BF)
        for k in range(2):

            @pl.when(fin_self(k))
            def _():
                fr[g, zh] = rb[g, k]

            @pl.when(jnp.logical_not(fin_self(k)))
            def _():
                d_copy(g, k).start()

    def finish_waits(g):
        for s in range(2):

            @pl.when(jnp.logical_not(jnp.logical_and(origin, zh == s)))
            def _():
                pltpu.make_async_remote_copy(
                    src_ref=fr.at[g, s],
                    dst_ref=fr.at[g, s],
                    send_sem=dsend.at[g * 2],
                    recv_sem=drecv.at[g * 2 + s],
                    device_id=cp,
                    device_id_type=MESH,
                ).wait_recv()

    def finish(g):
        finish_waits(g)
        gw_ref[:, g * CW : (g + 1) * CW] = fr[g, 0].astype(F32) + fr[g, 1].astype(F32)

    def f_copy(peer):
        return pltpu.make_async_remote_copy(
            src_ref=pvs.at[peer],
            dst_ref=pvr.at[d],
            send_sem=fsend.at[peer],
            recv_sem=frecv.at[d],
            device_id=at(peer, t),
            device_id_type=MESH,
        )

    def f_start(i, c):
        f_copy((d + i) % NDP).start()
        return c

    def f_wait(i, c):
        p = (d + i) % NDP
        pltpu.make_async_remote_copy(
            src_ref=pvr.at[p],
            dst_ref=pvr.at[p],
            send_sem=fsend.at[p],
            recv_sem=frecv.at[p],
            device_id=at(p, t),
            device_id_type=MESH,
        ).wait_recv()
        return c

    lax.fori_loop(1, NDP, e_start, 0, unroll=True)
    second(0)
    def turn(i, c):
        cols = pl.ds(pl.multiple_of(i * CW, CW), CW)
        xt[cols, :] = x[:, cols].T
        return c

    lax.fori_loop(0, 4, turn, 0)
    row = lax.broadcasted_iota(jnp.int32, (RB, 1), 0)
    slot = jnp.zeros((RB, 1), jnp.int32)
    length = jnp.ones((RB, 1), F32)
    advantage = jnp.zeros((RB, 1), F32)
    first = jnp.int32(0)
    for s in range(16):
        n = len_ref[0, 0, s]
        inside = jnp.logical_and(row >= first, row < first + n)
        slot = jnp.where(inside, row - first + bin_ref[0, 0, s] * SPAN, slot)
        length = jnp.where(inside, n.astype(F32), length)
        advantage = jnp.where(inside, adv_ref[0, 0, s], advantage)
        first = first + n
    importance = jnp.minimum(jnp.exp(to_col(gap_ref[...])), 2.0)
    coef_adv = (advantage * importance / length).astype(BF).astype(F32)
    coef_pull = (BETA / length).astype(BF).astype(F32)
    pick = (
        jnp.broadcast_to(slot, (RB, NDP * SPAN))
        == lax.broadcasted_iota(jnp.int32, (RB, NDP * SPAN), 1)
    ).astype(BF)
    slot_row = to_row(slot.astype(F32))
    place = (
        lax.broadcasted_iota(jnp.int32, (NDP * SPAN, RB), 0).astype(F32)
        == jnp.broadcast_to(slot_row, (NDP * SPAN, RB))
    ).astype(BF)

    w_share(0)
    policy(0)
    start(2)
    third(0)
    second(1)
    w_share(1)
    policy(1)
    start(3)
    second(2)
    finish_unit(0)
    third(1)
    third(2)

    def p_wait(i, c):
        p = (t + i) % 8
        pltpu.make_async_remote_copy(
            src_ref=pow_r.at[p],
            dst_ref=pow_r.at[p],
            send_sem=psend.at[p],
            recv_sem=precv.at[p],
            device_id=at(d, p),
            device_id_type=MESH,
        ).wait_recv()
        return c

    lax.fori_loop(1, 8, p_wait, 0)
    power = pow_r[0]
    for k in range(1, 8):
        power = power + pow_r[k]
    scale = to_col(lax.rsqrt(power[0:1, :] * (1.0 / WIDTH) + EPS))

    second(3)

    ld_cot.wait()

    def e_wait(i, c):
        p = (d + i) % NDP
        pltpu.make_async_remote_copy(
            src_ref=cr.at[p],
            dst_ref=cr.at[p],
            send_sem=esend.at[p],
            recv_sem=erecv.at[p],
            device_id=at(p, t),
            device_id_type=MESH,
        ).wait_recv()
        return c

    lax.fori_loop(1, NDP, e_wait, 0)

    finish_unit(2)
    slopes(0)
    finish_unit(1)
    spread(0)
    third(3)
    finish_unit(3)
    slopes(1)
    spread_far(0)
    spread(1)
    spread_end(0)
    reduce_core(0)
    spread_far(1)
    reduce_x(0)
    pvr[d] = pvs[d]
    lax.fori_loop(1, NDP, f_start, 0, unroll=True)
    spread_end(1)
    reduce_core(1)
    to_owner(0)
    reduce_x(1)
    to_owner(1)
    lax.fori_loop(1, NDP, f_wait, 0)
    pv_ref[0, 0] = pvr[...].reshape(NDP * SPAN, VW)
    finish(0)
    finish(1)

    for c in sent:
        c.wait_send()

    w_sent(0)
    w_sent(1)

    def p_done(i, c):
        p_copy((t + i) % 8).wait_send()
        return c

    def ef_done(i, c):
        e_copy((d + i) % NDP).wait_send()
        f_copy((d + i) % NDP).wait_send()
        return c

    lax.fori_loop(1, 8, p_done, 0)
    lax.fori_loop(1, NDP, ef_done, 0)
    for g in range(NG):
        for k in range(2):

            @pl.when(jnp.logical_not(fin_self(k)))
            def _():
                d_copy(g, k).wait_send()


def hand_over(packed_ref, grads_ref, pv_ref, gw_ref):
    pv_ref[...] = packed_ref[...]
    gw_ref[...] = grads_ref[...]


def on_device(
    tokens,
    ref_gain,
    ref_weight,
    pol_gain,
    pol_weight,
    lengths,
    bins,
    advantage,
    logprob_gap,
    cotangent,
):
    any_spec = pl.BlockSpec(memory_space=pl.ANY)
    vmem = pl.BlockSpec(memory_space=pltpu.VMEM)
    smem = pl.BlockSpec(memory_space=pltpu.SMEM)
    dma = pltpu.SemaphoreType.DMA

    def buf(*shape, dtype=BF):
        return pltpu.VMEM(shape, dtype)

    packed, grads = pl.pallas_call(
        kernel,
        out_shape=(
            jax.ShapeDtypeStruct(cotangent.shape, BF),
            jax.ShapeDtypeStruct((CHUNK, VW), F32),
        ),
        in_specs=[any_spec] * 4 + [vmem, vmem, smem, smem, smem, vmem],
        out_specs=(vmem, vmem),
        scratch_shapes=[
            buf(1024, FEAT),
            buf(FEAT, 1024),
            buf(FEAT, VW),
            buf(NG, FEAT, CW),
            buf(512, VW),
            buf(NG, FEAT, CW),
            buf(NG, FEAT, CW),
            buf(FEAT, 1, dtype=F32),
            buf(4, 2, 4, RB, CW),
            buf(4, 2, 2, HB, CW),
            buf(4, 2, 2, HB, CW),
            buf(4, 2, 2, HB, CW),
            buf(4, 3, 2, RB, CW),
            buf(4, 2, 2, HB, CW),
            buf(4, RB, CW),
            buf(4, RB, CW),
            buf(4, RB, CW, dtype=F32),
            buf(4, 4, RB, CW),
            buf(4, 4, RB, CW),
            buf(4, 2, HB, CW),
            buf(4, 2, HB, CW),
            buf(4, 2, HB, CW),
            buf(4, 2, HB, CW),
            buf(RB, VW, dtype=F32),
            buf(RB, VW, dtype=F32),
            buf(8, 8, RB, dtype=F32),
            buf(8, 8, RB, dtype=F32),
            buf(NDP, SPAN, VW),
            buf(NG, 2, 4, RB, CW),
            buf(NG, 2, 8, CHUNK, CW),
            buf(NG, 8, CHUNK, CW),
            buf(NG, 8, CHUNK, CW),
            buf(NG, 3, 2, CHUNK, CW),
            buf(NG, 2, CHUNK, CW),
            buf(NG, 2, CHUNK, CW),
            buf(NDP, SPAN, VW),
            buf(NDP, SPAN, VW),
            dma((4,)),
            dma((96,)),
            dma((96,)),
            dma((NG * 8,)),
            dma((NG * 8,)),
            dma((8,)),
            dma((8,)),
            dma((NDP,)),
            dma((NDP,)),
            dma((NDP,)),
            dma((NDP,)),
            dma((4,)),
            dma((4,)),
        ],
        compiler_params=pltpu.CompilerParams(collective_id=0, has_side_effects=True),
    )(
        tokens,
        ref_weight,
        pol_weight,
        cotangent,
        ref_gain.reshape(8, RB),
        pol_gain.reshape(8, 8, RB),
        lengths,
        bins,
        advantage,
        logprob_gap.reshape(1, RB),
    )
    return pl.pallas_call(
        hand_over,
        out_shape=(
            jax.ShapeDtypeStruct(cotangent.shape, BF),
            jax.ShapeDtypeStruct((CHUNK, VW), F32),
        ),
        in_specs=[vmem, vmem],
        out_specs=(vmem, vmem),
    )(packed, grads)


def solution(mesh):
    in_specs = (
        P("dp", "tensor"),
        P("tensor"),
        P("tensor", None),
        P(),
        P("dp", None),
        P("dp", "tensor", None),
        P("dp", "tensor", None),
        P("dp", "tensor", None),
        P(("dp", "tensor")),
        P("dp", "tensor", None, None),
    )
    out_specs = (P("dp", "tensor", None, None), P(("dp", "tensor"), None))
    return jax.shard_map(
        on_device, mesh=mesh, in_specs=in_specs, out_specs=out_specs, check_vma=False
    )
```
